256 devices in a mesh: pairs: 64 (over y, z, core), orb: 4 (over x).
Axes of the slice: x: 4, y: 4, z: 8, core: 2. Of those that a mesh axis runs over, the one named last changes fastest.
Arguments:
- amplitudes: float32 [1024, 128, 128], P(('pairs', 'orb')), may hold values from -4 to 4
- integrals: bfloat16 [1024, 128, 128], P(('pairs', 'orb')), may hold values from -6 to 6
- energies: float32 [1024, 128], P(('pairs', 'orb')), may hold values from 0.5 to 4
- intersections: bfloat16 [1024, 16, 128, 128], P(('pairs', 'orb')), may hold values from -0.5 to 0.5
- couplings: float32 [1024, 16], P(('pairs', 'orb')), may hold values from -2 to 2
- projector: float32 [1024, 128], P(('pairs', 'orb')), may hold values from -0.5 to 0.5
- pair_orbitals: int32 [1024, 2], P(('pairs', 'orb')), may hold values from 0 to 31
- coupled: int32 [1024, 16], replicated, may hold values from 0 to 1023, as said below
- pair_slot: int32 [1024], replicated, may hold values from 0 to 1023, as said below
Outputs:
- final_amplitudes: float32 [1024, 128, 128], P(('pairs', 'orb'))
- residual: float32 [1024, 128, 128], P(('pairs', 'orb'))
The draws below stay inside these ranges and needn't reach their ends.
Inputs may be any that keep to these rules, and one draw needn't show every extreme that they name: `coupled`: each row holds 16 different pair ids, never the id of the pair held in that row's slot. The rows of one device name at most 1 different pairs held by the devices of any one pairs index, and exactly 1 held by the devices of the next pairs index. `pair_slot`: A permutation of the pair ids.
All inputs are finite; a program needn't handle non-finite values.
Results may differ from the reference program's by a relative error of at most 0.00037.
Values may be sent and summed in bfloat16 or wider, within the bound.
A program may use at most 64 MiB of HBM per device.

```python
import math
import jax
import jax.numpy as jnp
from jax import lax

NV = 128
NB = 16
ITERS = 2
PAIRS_DEV = 4
TOTAL = 1024
NOCC = 32
CAP = 1
N_PAIRS = 64
N_ORB = 4


def plan_coupling(key):
    base_key = jax.random.fold_in(key, 31)
    key_perm, key_pick, key_score = jax.random.split(base_key, 3)
    devices = TOTAL // PAIRS_DEV
    group = PAIRS_DEV * N_ORB
    slot_of = jax.random.permutation(key_perm, TOTAL).astype(jnp.int32)
    pair_of = jnp.argsort(slot_of).astype(jnp.int32)
    jitter = jax.random.randint(key_pick, (devices, N_PAIRS, group), 0, 2 ** 20) * group + jnp.arange(group)
    chosen = jnp.argsort(jitter, axis=2)[:, :, :CAP].astype(jnp.int32)
    candidate = (jnp.arange(N_PAIRS)[None, :, None] * group + chosen).reshape(devices, N_PAIRS * CAP)
    columns = N_PAIRS * CAP
    scores = jax.random.randint(key_score, (TOTAL, columns), 0, 2 ** 20) * columns + jnp.arange(columns)
    row_ids = jnp.arange(TOTAL)
    owner_dev = row_ids // PAIRS_DEV
    owner_group = owner_dev // N_ORB
    row_cand = candidate[owner_dev]
    source = jnp.arange(columns) // CAP
    forced = (row_ids % PAIRS_DEV == 0)[:, None] & (source[None, :] == ((owner_group + 1) % N_PAIRS)[:, None])
    scores = jnp.where(forced, scores + 2 ** 30, scores)
    scores = jnp.where(row_cand == row_ids[:, None], -1, scores)
    top_vals, picked = lax.top_k(scores, NB)
    neighbour = jnp.take_along_axis(row_cand, picked, axis=1)
    return (slot_of, pair_of[neighbour].astype(jnp.int32))


def draw_coupled(key, part):
    return plan_coupling(key)[1]


def draw_pair_slot(key, part):
    return plan_coupling(key)[0]


def place_ends(result, stream_key, low, high):
    index_at = [jax.random.randint(jax.random.fold_in(stream_key, axis), (), 0, length) for axis, length in enumerate(result.shape)]
    widest = result.shape.index(max(result.shape))
    beside = index_at[:widest] + [(index_at[widest] + 1) % result.shape[widest]] + index_at[widest + 1:]
    return result.at[tuple(index_at)].set(low).at[tuple(beside)].set(high)


def block_scale(key, extent, cuts, low, largest):
    loudness, own = 1.0, jax.random.fold_in(key, 6)
    for dim, parts in cuts:
        heights = jnp.exp(jax.random.uniform(jax.random.fold_in(own, dim), (parts,), jnp.float32, low / len(cuts), largest / len(cuts)))
        loudness = loudness * jnp.repeat(heights, extent[dim] // parts).reshape([-1 if axis == dim else 1 for axis in range(len(extent))])
    return loudness


def normal_values(rng, dims, deviation, reach, shards=(), held_as=jnp.bfloat16):
    level = block_scale(rng, dims, shards, -0.22, 0.18) if shards else 1.0
    entries = jax.random.normal(rng, dims, jnp.float32) * deviation * level
    return jnp.minimum(jnp.maximum(entries, -reach), reach).astype(held_as)


def setup_inputs(seed: int = 0) -> dict:
    keys = jax.random.split(jax.random.key(seed), 10)
    return {
        "amplitudes": normal_values(keys[0], (TOTAL, NV, NV), 0.3, 4.0, ((0, 256),), jnp.float32),
        "integrals": normal_values(keys[1], (TOTAL, NV, NV), 1.0, 6.0, ((0, 256),)),
        "energies": jnp.clip(jnp.exp(math.log(4.0) - 2.0794415 * jax.random.uniform(keys[2], (TOTAL, NV), jnp.float32) ** block_scale(keys[2], (TOTAL, NV), ((0, 256),), -0.2, 0.2)), 0.5, 4.0),
        "intersections": normal_values(keys[3], (TOTAL, NB, NV, NV), NV ** -0.5, 0.5, ((0, 256),)),
        "couplings": normal_values(keys[4], (TOTAL, NB), 0.15, 2.0, ((0, 256),), jnp.float32),
        "projector": normal_values(keys[5], (TOTAL, NV), NV ** -0.5, 0.5, ((0, 256),), jnp.float32),
        "pair_orbitals": place_ends(jax.random.randint(keys[6], (TOTAL, 2), 0, NOCC), jax.random.fold_in(keys[6], 1), 0, NOCC - 1).astype(jnp.int32),
        "coupled": draw_coupled(jax.random.fold_in(keys[9], 71), 0),
        "pair_slot": draw_pair_slot(jax.random.fold_in(keys[9], 71), 0),
    }


def reference(amplitudes, integrals, energies, intersections, couplings, projector, pair_orbitals, coupled, pair_slot):
    highest = lax.Precision.HIGHEST
    neighbour = pair_slot[coupled].astype(jnp.int32)
    orbital_ids = jnp.arange(NOCC).astype(jnp.int32)
    first_hot = (pair_orbitals[:, 0:1] == orbital_ids[None, :]).astype(jnp.float32)
    second_hot = (pair_orbitals[:, 1:2] == orbital_ids[None, :]).astype(jnp.float32)
    denom = energies[:, :, None] + energies[:, None, :]
    state = amplitudes
    residual = amplitudes
    for step in range(ITERS):
        blocks = state.astype(jnp.bfloat16)
        blocks = lax.optimization_barrier(blocks)

        def couple_one(items):
            intersection, coeff, index = items
            near = blocks[index].astype(jnp.float32)
            wide = intersection.astype(jnp.float32)
            lifted = jnp.einsum("kab,kbc->kac", wide, near, precision=highest)
            scaled = (coeff[:, None, None] * lifted).astype(jnp.bfloat16)
            scaled = lax.optimization_barrier(scaled).astype(jnp.float32)
            return jnp.einsum("kac,kdc->ad", scaled, wide, precision=highest)

        coupling = lax.map(couple_one, (intersections, couplings, neighbour))
        projected = jnp.einsum("pab,pb->pa", state, projector, precision=highest)
        singles = jnp.dot(first_hot.T, projected, precision=highest) + jnp.dot(second_hot.T, projected, precision=highest)
        left = jnp.dot(first_hot, singles, precision=highest)
        right = jnp.dot(second_hot, singles, precision=highest)
        residual = (integrals.astype(jnp.float32) + energies[:, :, None] * state + state * energies[:, None, :]
                    - coupling + left[:, :, None] * projector[:, None, :] + projector[:, :, None] * right[:, None, :])
        state = state - residual / denom
    return state, residual
```

```python
import functools

import jax
import jax.numpy as jnp
from jax import lax
from jax.experimental import pallas as pl
from jax.experimental.pallas import tpu as pltpu
from jax.sharding import PartitionSpec as P

ITERS = 2
NOCC = 32
NX, NY, NZ, NC = 4, 4, 8, 2
MESH = pl.DeviceIdType.MESH
HIGHEST = lax.Precision.HIGHEST
DESTS = [(dy, dc) for dy in range(NY) for dc in range(NC)]


def pair_index(y, z, c):
    return (y * NZ + z) * NC + c


def tables(coupled, pair_slot, per_device):
    pair_idx = lax.axis_index("pairs")
    x = lax.axis_index("orb")
    y, z, c = pair_idx // (NZ * NC), pair_idx // NC % NZ, pair_idx % NC
    total = pair_slot.shape[0]
    group = NX * per_device
    back = jnp.arange(NZ, dtype=jnp.int32)
    source = pair_index(y, (z - back) % NZ, c)
    slots = source[:, None] * group + jnp.arange(group, dtype=jnp.int32)[None, :]
    ids = jnp.arange(total, dtype=jnp.int32)
    held = jnp.sum(
        jnp.where(pair_slot[None, None, :] == slots[:, :, None], ids[None, None, :], 0), axis=2
    )
    dy = jnp.arange(NY * NC, dtype=jnp.int32) // NC
    dc = jnp.arange(NY * NC, dtype=jnp.int32) % NC
    receiver = pair_index((y + dy) % NY, z, (c + dc) % NC) * NX + x
    rows = (receiver[:, None] * per_device + jnp.arange(per_device, dtype=jnp.int32)[None, :]).reshape(-1)
    wanted = coupled[rows].reshape(NY * NC, -1)
    place = jnp.arange(group, dtype=jnp.int32)
    place = (place // per_device - x) % NX * per_device + place % per_device
    select = jnp.max(
        jnp.where(
            held[:, None, :, None] == wanted[None, :, None, :], place[None, None, :, None], 0
        ),
        axis=(2, 3),
    )
    target = pair_slot[wanted[0]] // group
    ty, tz, tc = target // (NZ * NC), target // NC % NZ, target % NC
    entry = (((y - ty) % NY) * NC + (c + tc) % NC) * NZ + (z - tz) % NZ
    return select.reshape(-1), entry


def kernel(
    select, entry, orbs, coup, amp, integ_hbm, ener, inter_hbm, proj, fin, res,
    *scratch,
):
    gath = [scratch[0:NZ], scratch[NZ : 2 * NZ]]
    out_buf = scratch[2 * NZ : 2 * NZ + 2]
    recv = scratch[2 * NZ + 2 : 2 * NZ + 4]
    (parts, part_y, part_x, part_z, inter, integ, state, den, pcol, base, local_sem, blk_send, blk_recv,
     y_send, y_recv, p_send, p_recv) = scratch[2 * NZ + 4 :]
    per = amp.shape[0]
    width = amp.shape[1]
    nb = inter.shape[0] // per
    pair_idx = lax.axis_index("pairs")
    x = lax.axis_index("orb")
    y, z, c = pair_idx // (NZ * NC), lax.rem(pair_idx // NC, NZ), lax.rem(pair_idx, NC)

    def dev(dx=0, dy=0, dz=0, dc=0):
        return (
            pair_index(lax.rem(y + dy, NY), lax.rem(z + dz, NZ), lax.rem(c + dc, NC)),
            lax.rem(x + dx, NX),
        )

    inter_copy = pltpu.make_async_copy(inter_hbm, inter, local_sem.at[0])
    integ_copy = pltpu.make_async_copy(integ_hbm, integ, local_sem.at[1])
    inter_copy.start()
    integ_copy.start()

    peers = [dev(dx=d) for d in range(1, NX)]
    peers += [dev(dy=dy, dc=dc) for dy, dc in DESTS[1:]]
    peers += [dev(dz=d) for d in range(1, NZ)]
    barrier = pltpu.get_barrier_semaphore()
    for peer in peers:
        pl.semaphore_signal(barrier, inc=1, device_id=peer, device_id_type=MESH)

    for s in range(per):
        state[s] = amp[s]
        gath[0][0][s] = amp[s].astype(jnp.bfloat16)
    pl.semaphore_wait(barrier, len(peers))

    sent = []

    def send(src, dst, ssem, rsem, to):
        copy = pltpu.make_async_remote_copy(
            src_ref=src, dst_ref=dst, send_sem=ssem, recv_sem=rsem, device_id=to, device_id_type=MESH
        )
        copy.start()
        sent.append(copy)

    def arrived(ref, sem):
        pltpu.make_async_copy(ref, ref, sem).wait()

    def column(row):
        return jnp.broadcast_to(row, (width, width)).T

    for it in range(ITERS):
        g = gath[it]
        sems = blk_recv.at[it]

        def part(k, q, g=g):
            return g[k].at[pl.ds(q * per, per)]

        def push(k, q, k2, q2, to, sems=sems, part=part, it=it):
            send(part(k, q), part(k2, q2), blk_send.at[it], sems.at[q2 * NZ + k2], to)

        def ready(k, q, sems=sems, part=part):
            arrived(part(k, q), sems.at[q * NZ + k])

        def deliver(k, it=it, g=g, ready=ready):
            ready(k, 2)
            ready(k, 3)
            for i, (dy, dc) in enumerate(DESTS):
                block = g[k][select[k * len(DESTS) + i]]
                if i == 0:
                    recv[it][k] = block
                else:
                    out_buf[it][k * (len(DESTS) - 1) + i - 1] = block
            for i, (dy, dc) in enumerate(DESTS):
                if i:
                    send(
                        out_buf[it].at[k * (len(DESTS) - 1) + i - 1],
                        recv[it].at[i * NZ + k],
                        y_send.at[it],
                        y_recv.at[it],
                        dev(dy=dy, dc=dc),
                    )

        up, down, right, left = dev(dz=1), dev(dz=NZ - 1), dev(dx=1), dev(dx=NX - 1)
        push(0, 0, 1, 0, up)
        push(0, 0, 7, 0, down)
        push(0, 0, 0, 1, left)
        push(0, 0, 0, 3, right)

        orbital = lax.broadcasted_iota(jnp.int32, (NOCC, width), 0)
        total = jnp.zeros((NOCC, width), jnp.float32)
        for s in range(per):
            row = lax.dot_general(
                jnp.broadcast_to(proj[s : s + 1, :], (8, width)),
                state[s],
                (((1,), (1,)), ((), ())),
                precision=HIGHEST,
                preferred_element_type=jnp.float32,
            )[0:1]
            row = jnp.broadcast_to(row, (NOCC, width))
            total += jnp.where(orbital == orbs[2 * s], row, 0.0)
            total += jnp.where(orbital == orbs[2 * s + 1], row, 0.0)
        p = parts.at[it]
        p[0] = total
        for i, (dy, dc) in enumerate(DESTS):
            if i:
                send(p.at[0], part_y.at[it, i - 1], p_send.at[it], p_recv.at[it, 0], dev(dy=dy, dc=dc))

        ready(0, 1)
        push(0, 1, 1, 1, up)
        push(0, 1, 7, 1, down)
        push(0, 1, 0, 2, left)

        if it == 0:
            integ_copy.wait()
            for s in range(per):
                e_row = ener[s : s + 1, :]
                den[s] = column(e_row) + e_row
                pcol[s] = column(proj[s : s + 1, :])
        for s in range(per):
            base[s] = integ[s].astype(jnp.float32) + den[s] * state[s]

        for q, (f, to) in enumerate(((3, right), (2, left))):
            ready(1, q)
            push(1, q, 2, q, up)
            ready(7, q)
            push(7, q, 6, q, down)
            push(1, q, 1, f, to)
            push(7, q, 7, f, to)

        arrived(part_y.at[it], p_recv.at[it, 0])
        total = p[0]
        for i in range(len(DESTS) - 1):
            total += part_y[it, i]
        p[1] = total
        for d in range(1, NX):
            send(p.at[1], part_x.at[it, d - 1], p_send.at[it], p_recv.at[it, 1], dev(dx=d))

        deliver(0)
        for q, (f, to) in enumerate(((3, right), (2, left))):
            ready(2, q)
            push(2, q, 3, q, up)
            ready(6, q)
            push(6, q, 5, q, down)
            push(2, q, 2, f, to)
            push(6, q, 6, f, to)
        deliver(1)
        deliver(7)

        arrived(part_x.at[it], p_recv.at[it, 1])
        total = p[1]
        for i in range(NX - 1):
            total += part_x[it, i]
        p[2] = total
        for d in range(1, NZ):
            send(p.at[2], part_z.at[it, d - 1], p_send.at[it], p_recv.at[it, 2], dev(dz=d))

        for q, (f, to) in enumerate(((3, right), (2, left))):
            ready(3, q)
            ready(5, q)
            if q == 0:
                push(3, q, 4, q, up)
            else:
                push(5, q, 4, q, down)
            push(3, q, 3, f, to)
            push(5, q, 5, f, to)
        deliver(2)
        deliver(6)
        ready(4, 0)
        push(4, 0, 4, 3, right)
        ready(4, 1)
        push(4, 1, 4, 2, left)
        deliver(3)
        deliver(5)
        deliver(4)

        arrived(part_z.at[it], p_recv.at[it, 2])
        total = p[2]
        for i in range(NZ - 1):
            total += part_z[it, i]
        p[3] = total

        if it == 0:
            inter_copy.wait()
        arrived(recv[it].at[pl.ds(NZ, (len(DESTS) - 1) * NZ)], y_recv.at[it])

        def one_slot(s, carry, it=it, p=p):
            acc = jnp.zeros((width, width), jnp.float32)
            for k in range(nb):
                own = inter[s * nb + k]
                lifted = jnp.dot(own, recv[it][entry[s * nb + k]], preferred_element_type=jnp.float32)
                scaled = (coup[s * nb + k] * lifted).astype(jnp.bfloat16)
                acc += lax.dot_general(
                    scaled, own, (((1,), (1,)), ((), ())), preferred_element_type=jnp.float32
                )
            left_row = p[3, pl.ds(orbs[2 * s], 1), :]
            right_row = p[3, pl.ds(orbs[2 * s + 1], 1), :]
            resid = (
                base[s] - acc + column(left_row) * proj[pl.ds(s, 1), :] + pcol[s] * right_row
            )
            new = state[s] - resid / den[s]
            if it == ITERS - 1:
                res[s] = resid
                fin[s] = new
            else:
                state[s] = new
                gath[it + 1][0][s] = new.astype(jnp.bfloat16)
            return carry

        lax.fori_loop(0, per, one_slot, 0)

    for copy in sent:
        copy.wait_send()


def body(amplitudes, integrals, energies, intersections, couplings, projector, pair_orbitals, coupled, pair_slot):
    per, width, _ = amplitudes.shape
    nb = coupled.shape[1]
    group = NX * per
    receivers = len(DESTS)
    select, entry = tables(coupled, pair_slot, per)
    bf16, f32 = jnp.bfloat16, jnp.float32
    vmem = pl.BlockSpec(memory_space=pltpu.VMEM)
    smem = pl.BlockSpec(memory_space=pltpu.SMEM)
    hbm = pl.BlockSpec(memory_space=pl.ANY)
    dma = pltpu.SemaphoreType.DMA
    square = (per, width, width)
    scratch = [pltpu.VMEM((group, width, width), bf16) for _ in range(2 * NZ)]
    scratch += [pltpu.VMEM((NZ * (receivers - 1), width, width), bf16) for _ in range(2)]
    scratch += [pltpu.VMEM((NZ * receivers, width, width), bf16) for _ in range(2)]
    scratch += [
        pltpu.VMEM((ITERS, 4, NOCC, width), f32),
        pltpu.VMEM((ITERS, receivers - 1, NOCC, width), f32),
        pltpu.VMEM((ITERS, NX - 1, NOCC, width), f32),
        pltpu.VMEM((ITERS, NZ - 1, NOCC, width), f32),
        pltpu.VMEM((per * nb, width, width), bf16),
        pltpu.VMEM(square, bf16),
        pltpu.VMEM(square, f32),
        pltpu.VMEM(square, f32),
        pltpu.VMEM(square, f32),
        pltpu.VMEM(square, f32),
        dma((2,)),
        dma((ITERS,)),
        dma((ITERS, 4 * NZ)),
        dma((ITERS,)),
        dma((ITERS,)),
        dma((ITERS,)),
        dma((ITERS, 3)),
    ]
    return pl.pallas_call(
        kernel,
        out_shape=(
            jax.ShapeDtypeStruct(square, f32),
            jax.ShapeDtypeStruct(square, f32),
        ),
        in_specs=[smem, smem, smem, smem, vmem, hbm, vmem, hbm, vmem],
        out_specs=(vmem, vmem),
        scratch_shapes=scratch,
        compiler_params=pltpu.CompilerParams(
            collective_id=0, has_side_effects=True, vmem_limit_bytes=48 * 1024 * 1024
        ),
    )(
        select,
        entry,
        pair_orbitals.reshape(-1),
        couplings.reshape(-1),
        amplitudes,
        integrals,
        energies,
        intersections.reshape(per * nb, width, width),
        projector,
    )


def solution(mesh):
    both = ("pairs", "orb")
    return jax.shard_map(
        body,
        mesh=mesh,
        in_specs=(
            P(both, None, None),
            P(both, None, None),
            P(both, None),
            P(both, None, None, None),
            P(both, None),
            P(both, None),
            P(both, None),
            P(),
            P(),
        ),
        out_specs=(P(both, None, None), P(both, None, None)),
        check_vma=False,
    )
```

```python
import jax
import jax.numpy as jnp
from jax import lax
from jax.experimental import pallas as pl
from jax.experimental.pallas import tpu as pltpu
from jax.sharding import PartitionSpec as P

ITERS = 2
NOCC = 32
NX, NY, NZ, NC = 4, 4, 8, 2
PLANE = NX * NY * NC
MESH = pl.DeviceIdType.MESH
HIGHEST = lax.Precision.HIGHEST
ROUNDS = ((0,), (1, 7), (2, 6), (3, 5), (4,))
FIRST = {0: 0, 1: 1, 2: 3, 3: 5, 4: 7}


def pair_index(y, z, c):
    return (y * NZ + z) * NC + c


def kernel(
    coup, orbs, slot_of, amp_hbm, integ_hbm, ener_hbm, inter_hbm, proj_hbm, coupled_hbm, slots_hbm, fin, res,
    *scratch,
):
    gath = [scratch[0:NZ], scratch[NZ : 2 * NZ]]
    out_buf = scratch[2 * NZ : 2 * NZ + 2]
    recv = scratch[2 * NZ + 2 : 2 * NZ + 4]
    blocks = scratch[2 * NZ + 4 : 2 * NZ + 6]
    (parts, full, half, part_y, part_x, part_z, sums, inter, integ, state, ener, proj, cpl, slots, den, pcol, base,
     sel_v, want_v, sel, want, entry,
     local_sem, x_send, x_recv, z_send, z_recv, y_send, y_recv, p_send, p_recv) = scratch[2 * NZ + 6 :]
    per, width, _ = state.shape
    nb = inter.shape[0] // per
    group = NX * per
    quarter = width // NX
    pair_idx = lax.axis_index("pairs")
    x = lax.axis_index("orb")
    y, z, c = pair_idx // (NZ * NC), pair_idx // NC % NZ, pair_idx % NC

    xs = [(x + d) % NX for d in range(NX)]
    ys = [(y + d) % NY for d in range(NY)]
    zs = [(z + d) % NZ for d in range(NZ)]
    cs = [(c + d) % NC for d in range(NC)]

    def dev(dx=0, dy=0, dz=0, dc=0):
        return (pair_index(ys[dy], zs[dz], cs[dc]), xs[dx])

    steps = [(dx, dy, dc) for dx in range(NX) for dy in range(NY) for dc in range(NC)]

    local = [
        pltpu.make_async_copy(a, b, local_sem.at[i])
        for i, (a, b) in enumerate(
            (
                (amp_hbm, state),
                (coupled_hbm, cpl),
                (slots_hbm, slots),
                (proj_hbm, proj),
                (ener_hbm, ener),
                (integ_hbm, integ),
                (inter_hbm, inter),
            )
        )
    ]
    for copy in local:
        copy.start()

    barrier = pltpu.get_barrier_semaphore()

    for d in range(1, NZ):
        pl.semaphore_signal(barrier, inc=1, device_id=dev(dz=d), device_id_type=MESH)
    for dx, dy, dc in steps[1:]:
        pl.semaphore_signal(barrier, inc=1, device_id=dev(dx, dy, 0, dc), device_id_type=MESH)

    local[0].wait()
    for s in range(per):
        blocks[0][s] = state[s].astype(jnp.bfloat16)

    sent = []

    def send(src, dst, ssem, rsem, to):
        copy = pltpu.make_async_remote_copy(
            src_ref=src, dst_ref=dst, send_sem=ssem, recv_sem=rsem, device_id=to, device_id_type=MESH
        )
        copy.start()
        return copy

    def arrived(ref, sem):
        pltpu.make_async_copy(ref, ref, sem).wait()

    def column(row):
        return jnp.broadcast_to(row, (width, width)).T

    def make_tables():
        local[1].wait()
        local[2].wait()
        lane = lax.broadcasted_iota(jnp.int32, (nb, width), 1)
        span = width // NY
        wanted = jnp.zeros((nb, width), jnp.int32)
        for yy in range(NY):
            start = pl.multiple_of(yy * (NZ * span) + z // NY * width, width)
            tile = cpl[:, pl.ds(start, width)]
            tile = pltpu.roll(tile, (yy * span + width - z % NY * span) % width, 1)
            wanted = jnp.where(lane // span == yy, tile, wanted)
        want_v[...] = wanted
        row = lax.broadcasted_iota(jnp.int32, (width, width), 0)
        col = lax.broadcasted_iota(jnp.int32, (width, width), 1)
        slot = pair_index(y, (z + NZ - row // group) % NZ, c) * group + row % group
        held = jnp.zeros((width, width), jnp.int32)
        for r in range(slots.shape[0]):
            held += jnp.where(slots[r : r + 1, :] == slot, col + r * width, 0)
        shift = width // 2
        while shift:
            held += pltpu.roll(held, shift, 1)
            shift //= 2
        hits = jnp.zeros((width, width), jnp.int32)
        for e in range(nb):
            hits = jnp.maximum(hits, jnp.where(wanted[e : e + 1, :] == held, row % group, 0))
        best = hits
        for r in range(1, per):
            best = jnp.maximum(best, pltpu.roll(hits, width - r, 1))
        sel_v[...] = jnp.max(best.reshape(NZ, group, width), axis=1)
        a = pltpu.make_async_copy(sel_v, sel, local_sem.at[len(local)])
        b = pltpu.make_async_copy(want_v, want, local_sem.at[len(local) + 1])
        a.start()
        b.start()
        a.wait()
        b.wait()

    def make_entries():
        mine = ((y * NC + c) * NX + x) * per

        def one(i, carry):
            t = slot_of[want[i % nb, mine + i // nb]] // group
            ty, tz, tc = t // (NZ * NC), t // NC % NZ, t % NC
            k = (z - tz + NZ) % NZ
            order = jnp.where(k <= NZ // 2, jnp.maximum(2 * k - 1, 0), 2 * (NZ - k))
            entry[i] = ((y - ty + NY) % NY * NC + (c + tc) % NC) * NZ + order
            return carry

        lax.fori_loop(0, per * nb, one, 0)

    own_rows = pl.ds(pl.multiple_of(x * quarter, quarter), quarter)

    def spread(it, s):
        for d in range(1, NX):
            theirs = pl.ds(pl.multiple_of(xs[d] * quarter, quarter), quarter)
            send(
                blocks[it].at[s, theirs],
                gath[it][0].at[x * per + s],
                x_send.at[it],
                x_recv.at[it],
                dev(dx=d),
            )
        gath[it][0][x * per + s] = blocks[it][s, own_rows, :]

    def singles_terms(it):
        if it == 0:
            local[3].wait()
        orbital = lax.broadcasted_iota(jnp.int32, (NOCC, width), 0)
        total = jnp.zeros((NOCC, width), jnp.float32)
        for s in range(per):
            row = lax.dot_general(
                jnp.broadcast_to(proj[s : s + 1, :], (8, width)),
                state[s],
                (((1,), (1,)), ((), ())),
                precision=HIGHEST,
                preferred_element_type=jnp.float32,
            )[0:1]
            row = jnp.broadcast_to(row, (NOCC, width))
            total += jnp.where(orbital == orbs[s, 0], row, 0.0)
            total += jnp.where(orbital == orbs[s, 1], row, 0.0)
        parts[it] = total

    for it in range(ITERS):
        g = gath[it]

        def push(k, h, k2, to, g=g, it=it):
            def part(j):
                return g[j].at[pl.ds(h * (group // 2), group // 2)]

            sent.append(send(part(k), part(k2), z_send.at[it], z_recv.at[it, k2 * 2 + h], to))

        def ready(k, h, g=g, it=it):
            arrived(g[k].at[pl.ds(h * (group // 2), group // 2)], z_recv.at[it, k * 2 + h])

        def deliver(ks, it=it, g=g):
            first, count = FIRST[ks[0]], len(ks)

            for i, (dx, dy, dc) in enumerate(steps):
                at = ((ys[dy] * NC + cs[dc]) * NX + xs[dx]) * per
                for j, k in enumerate(ks):
                    out_buf[it][i, first + j] = g[k][sel[k, at]]
            for j in range(count):
                recv[it][first + j, own_rows, :] = out_buf[it][0, first + j]
            for i, (dx, dy, dc) in enumerate(steps):
                if i:
                    send(
                        out_buf[it].at[i, pl.ds(first, count)],
                        recv[it].at[pl.ds((dy * NC + dc) * NZ + first, count), own_rows],
                        y_send.at[it],
                        y_recv.at[it],
                        dev(dx, dy, 0, dc),
                    )

        if it == 0:
            singles_terms(0)
            make_tables()
            pl.semaphore_wait(barrier, PLANE - 1 + NZ - 1)
            for s in range(per):
                spread(0, s)
        else:
            singles_terms(it)
        share = NOCC // NC
        mine = pl.ds(pl.multiple_of(c * share, share), share)
        other = pl.ds(pl.multiple_of((1 - c) * share, share), share)
        sent.append(send(parts.at[it, other], half.at[it], p_send.at[it, 0], p_recv.at[it, 0], dev(dc=1)))

        up, down = dev(dz=1), dev(dz=NZ - 1)
        arrived(g[0].at[pl.ds(0, group - per)], x_recv.at[it])
        for h in range(2):
            push(0, h, 1, up)
            push(0, h, 7, down)
        deliver((0,))

        arrived(half.at[it], p_recv.at[it, 0])
        sums[it, 0] = parts[it, mine, :] + half[it]
        for d in range(1, NY):
            sent.append(send(sums.at[it, 0], part_y.at[it, d - 1], p_send.at[it, 1], p_recv.at[it, 1], dev(dy=d)))

        for h in range(2):
            ready(1, h)
            push(1, h, 2, up)
            ready(7, h)
            push(7, h, 6, down)
        deliver((1, 7))

        arrived(part_y.at[it], p_recv.at[it, 1])
        sums[it, 1] = sums[it, 0] + part_y[it, 0] + part_y[it, 1] + part_y[it, 2]
        for d in range(1, NX):
            sent.append(send(sums.at[it, 1], part_x.at[it, d - 1], p_send.at[it, 2], p_recv.at[it, 2], dev(dx=d)))

        for h in range(2):
            ready(2, h)
            push(2, h, 3, up)
            ready(6, h)
            push(6, h, 5, down)
        deliver((2, 6))

        arrived(part_x.at[it], p_recv.at[it, 2])
        sums[it, 2] = sums[it, 1] + part_x[it, 0] + part_x[it, 1] + part_x[it, 2]
        for d in range(1, NZ):
            sent.append(send(sums.at[it, 2], part_z.at[it, d - 1], p_send.at[it, 3], p_recv.at[it, 3], dev(dz=d)))

        ready(3, 0)
        push(3, 0, 4, up)
        ready(5, 1)
        push(5, 1, 4, down)
        ready(5, 0)
        ready(3, 1)
        deliver((3, 5))
        ready(4, 0)
        ready(4, 1)
        deliver((4,))

        arrived(part_z.at[it], p_recv.at[it, 3])
        total = sums[it, 2]
        for i in range(NZ - 1):
            total += part_z[it, i]
        full[it, mine, :] = total
        sums[it, 3] = total
        sent.append(send(sums.at[it, 3], half.at[ITERS + it], p_send.at[it, 4], p_recv.at[it, 4], dev(dc=1)))

        if it == 0:
            make_entries()
            local[4].wait()
            local[5].wait()
            for s in range(per):
                e_row = ener[s : s + 1, :]
                den[s] = column(e_row) + e_row
                pcol[s] = column(proj[s : s + 1, :])
        for s in range(per):
            base[s] = integ[s].astype(jnp.float32) + den[s] * state[s]

        arrived(half.at[ITERS + it], p_recv.at[it, 4])
        full[it, other, :] = half[ITERS + it]
        if it == 0:
            local[6].wait()
        arrived(recv[it].at[pl.ds(0, (PLANE - 1) * NZ // NX)], y_recv.at[it])

        def one_slot(s, carry, it=it):
            acc = jnp.zeros((width, width), jnp.float32)
            for k in range(nb):
                own = inter[s * nb + k]
                lifted = jnp.dot(own, recv[it][entry[s * nb + k]], preferred_element_type=jnp.float32)
                scaled = (coup[s, k] * lifted).astype(jnp.bfloat16)
                acc += lax.dot_general(
                    scaled, own, (((1,), (1,)), ((), ())), preferred_element_type=jnp.float32
                )
            left_row = full[it, pl.ds(orbs[s, 0], 1), :]
            right_row = full[it, pl.ds(orbs[s, 1], 1), :]
            resid = base[s] - acc + column(left_row) * proj[pl.ds(s, 1), :] + pcol[s] * right_row
            new = state[s] - resid / den[s]
            if it == ITERS - 1:
                res[s] = resid
                fin[s] = new
            else:
                state[s] = new
                blocks[it + 1][s] = new.astype(jnp.bfloat16)
                spread(it + 1, s)
            return carry

        lax.fori_loop(0, per, one_slot, 0)

    for copy in sent:
        copy.wait_send()
    for it in range(ITERS):
        arrived(gath[it][0].at[pl.ds(0, group - per)], x_send.at[it])
        sends = recv[it].at[pl.ds(0, (PLANE - 1) * NZ // NX)]
        arrived(sends, y_send.at[it])


def body(amplitudes, integrals, energies, intersections, couplings, projector, pair_orbitals, coupled, pair_slot):
    per, width, _ = amplitudes.shape
    nb = coupled.shape[1]
    total = pair_slot.shape[0]
    group = NX * per
    quarter = width // NX
    bf16, f32, i32 = jnp.bfloat16, jnp.float32, jnp.int32
    vmem = pl.BlockSpec(memory_space=pltpu.VMEM)
    smem = pl.BlockSpec(memory_space=pltpu.SMEM)
    hbm = pl.BlockSpec(memory_space=pltpu.HBM)
    dma = pltpu.SemaphoreType.DMA
    square = (per, width, width)
    share = NOCC // NC
    scratch = [pltpu.VMEM((group, quarter, width), bf16) for _ in range(2 * NZ)]
    scratch += [pltpu.VMEM((PLANE, NZ, quarter, width), bf16) for _ in range(2)]
    scratch += [pltpu.VMEM((NZ * NY * NC, width, width), bf16) for _ in range(2)]
    scratch += [pltpu.VMEM(square, bf16) for _ in range(2)]
    scratch += [
        pltpu.VMEM((ITERS, NOCC, width), f32),
        pltpu.VMEM((ITERS, NOCC, width), f32),
        pltpu.VMEM((2 * ITERS, share, width), f32),
        pltpu.VMEM((ITERS, NY - 1, share, width), f32),
        pltpu.VMEM((ITERS, NX - 1, share, width), f32),
        pltpu.VMEM((ITERS, NZ - 1, share, width), f32),
        pltpu.VMEM((ITERS, 4, share, width), f32),
        pltpu.VMEM((per * nb, width, width), bf16),
        pltpu.VMEM(square, bf16),
        pltpu.VMEM(square, f32),
        pltpu.VMEM((per, width), f32),
        pltpu.VMEM((per, width), f32),
        pltpu.VMEM((nb, total), i32),
        pltpu.VMEM((total // width, width), i32),
        pltpu.VMEM(square, f32),
        pltpu.VMEM(square, f32),
        pltpu.VMEM(square, f32),
        pltpu.VMEM((NZ, width), i32),
        pltpu.VMEM((nb, width), i32),
        pltpu.SMEM((NZ, width), i32),
        pltpu.SMEM((nb, width), i32),
        pltpu.SMEM((per * nb,), i32),
        dma((9,)),
        dma((ITERS,)),
        dma((ITERS,)),
        dma((ITERS,)),
        dma((ITERS, 2 * NZ)),
        dma((ITERS,)),
        dma((ITERS,)),
        dma((ITERS, 5)),
        dma((ITERS, 5)),
    ]
    return pl.pallas_call(
        kernel,
        out_shape=(
            jax.ShapeDtypeStruct(square, f32),
            jax.ShapeDtypeStruct(square, f32),
        ),
        in_specs=[smem, smem, smem, hbm, hbm, hbm, hbm, hbm, hbm, hbm],
        out_specs=(vmem, vmem),
        scratch_shapes=scratch,
        compiler_params=pltpu.CompilerParams(
            collective_id=0, has_side_effects=True, vmem_limit_bytes=67043328
        ),
    )(
        couplings,
        pair_orbitals,
        pair_slot,
        amplitudes,
        integrals,
        energies,
        intersections.reshape(per * nb, width, width),
        projector,
        coupled.T,
        pair_slot.reshape(total // width, width),
    )


def solution(mesh):
    both = ("pairs", "orb")
    return jax.shard_map(
        body,
        mesh=mesh,
        in_specs=(
            P(both, None, None),
            P(both, None, None),
            P(both, None),
            P(both, None, None, None),
            P(both, None),
            P(both, None),
            P(both, None),
            P(),
            P(),
        ),
        out_specs=(P(both, None, None), P(both, None, None)),
        check_vma=False,
    )
```

```python
import jax
import jax.numpy as jnp
from jax import lax
from jax.experimental import pallas as pl
from jax.experimental.pallas import tpu as pltpu
from jax.sharding import PartitionSpec as P

ITERS = 2
NOCC = 32
NX, NY, NZ, NC = 4, 4, 8, 2
PLANE = NX * NY * NC
MESH = pl.DeviceIdType.MESH
HIGHEST = lax.Precision.HIGHEST
ROUNDS = ((0,), (1, 7), (2, 6), (3, 5), (4,))
FIRST = {0: 0, 1: 1, 2: 3, 3: 5, 4: 7}


def pair_index(y, z, c):
    return (y * NZ + z) * NC + c


def kernel(
    coup, orbs, slot_of, amp_hbm, integ_hbm, ener_hbm, inter_hbm, proj_hbm, coupled_hbm, slots_hbm, last_hbm, change_hbm,
    *scratch,
):
    gath = [scratch[0:NZ], scratch[NZ : 2 * NZ]]
    out_buf = scratch[2 * NZ : 2 * NZ + 2]
    recv = scratch[2 * NZ + 2 : 2 * NZ + 4]
    blocks = scratch[2 * NZ + 4 : 2 * NZ + 6]
    (parts, full, half, part_y, part_x, part_z, sums, inter, integ, state, ener, proj, cpl, slots, den, pcol, base, change,
     sel_v, want_v, sel, want, entry,
     local_sem, x_send, x_recv, z_send, z_recv, y_send, y_recv, p_send, p_recv) = scratch[2 * NZ + 6 :]
    per, width, _ = state.shape
    nb = inter.shape[0] // per
    group = NX * per
    quarter = width // NX
    pair_idx = lax.axis_index("pairs")
    x = lax.axis_index("orb")
    y, z, c = pair_idx // (NZ * NC), pair_idx // NC % NZ, pair_idx % NC

    xs = [(x + d) % NX for d in range(NX)]
    ys = [(y + d) % NY for d in range(NY)]
    zs = [(z + d) % NZ for d in range(NZ)]
    cs = [(c + d) % NC for d in range(NC)]

    def dev(dx=0, dy=0, dz=0, dc=0):
        return (pair_index(ys[dy], zs[dz], cs[dc]), xs[dx])

    steps = [(dx, dy, dc) for dx in range(NX) for dy in range(NY) for dc in range(NC)]
    far_first = sorted(steps, key=lambda t: -(min(t[0], NX - t[0]) + min(t[1], NY - t[1])))

    local = [
        pltpu.make_async_copy(a, b, local_sem.at[i])
        for i, (a, b) in enumerate(
            (
                (amp_hbm, state),
                (coupled_hbm, cpl),
                (slots_hbm, slots),
                (proj_hbm, proj),
                (ener_hbm, ener),
                (integ_hbm, integ),
                (inter_hbm, inter),
            )
        )
    ]
    for copy in local:
        copy.start()

    barrier = pltpu.get_barrier_semaphore()

    for d in range(1, NZ):
        pl.semaphore_signal(barrier, inc=1, device_id=dev(dz=d), device_id_type=MESH)
    for dx, dy, dc in steps[1:]:
        pl.semaphore_signal(barrier, inc=1, device_id=dev(dx, dy, 0, dc), device_id_type=MESH)

    local[0].wait()
    for s in range(per):
        blocks[0][s] = state[s].astype(jnp.bfloat16)

    sent = []

    def send(src, dst, ssem, rsem, to):
        copy = pltpu.make_async_remote_copy(
            src_ref=src, dst_ref=dst, send_sem=ssem, recv_sem=rsem, device_id=to, device_id_type=MESH
        )
        copy.start()
        return copy

    def arrived(ref, sem):
        pltpu.make_async_copy(ref, ref, sem).wait()

    def column(row):
        return jnp.broadcast_to(row, (width, width)).T

    def make_tables():
        local[1].wait()
        local[2].wait()
        lane = lax.broadcasted_iota(jnp.int32, (nb, width), 1)
        span = width // NY
        wanted = jnp.zeros((nb, width), jnp.int32)
        for yy in range(NY):
            start = pl.multiple_of(yy * (NZ * span) + z // NY * width, width)
            tile = cpl[:, pl.ds(start, width)]
            tile = pltpu.roll(tile, (yy * span + width - z % NY * span) % width, 1)
            wanted = jnp.where(lane // span == yy, tile, wanted)
        want_v[...] = wanted
        row = lax.broadcasted_iota(jnp.int32, (width, width), 0)
        col = lax.broadcasted_iota(jnp.int32, (width, width), 1)
        slot = pair_index(y, (z + NZ - row // group) % NZ, c) * group + row % group
        held = jnp.zeros((width, width), jnp.int32)
        for r in range(slots.shape[0]):
            held += jnp.where(slots[r : r + 1, :] == slot, col + r * width, 0)
        shift = width // 2
        while shift:
            held += pltpu.roll(held, shift, 1)
            shift //= 2
        hits = jnp.zeros((width, width), jnp.int32)
        for e in range(nb):
            hits = jnp.maximum(hits, jnp.where(wanted[e : e + 1, :] == held, row % group, 0))
        best = hits
        for r in range(1, per):
            best = jnp.maximum(best, pltpu.roll(hits, width - r, 1))
        sel_v[...] = jnp.max(best.reshape(NZ, group, width), axis=1)
        a = pltpu.make_async_copy(sel_v, sel, local_sem.at[len(local)])
        b = pltpu.make_async_copy(want_v, want, local_sem.at[len(local) + 1])
        a.start()
        b.start()
        a.wait()
        b.wait()

    def make_entries():
        mine = ((y * NC + c) * NX + x) * per

        def one(i, carry):
            t = slot_of[want[i % nb, mine + i // nb]] // group
            ty, tz, tc = t // (NZ * NC), t // NC % NZ, t % NC
            k = (z - tz + NZ) % NZ
            order = jnp.where(k <= NZ // 2, jnp.maximum(2 * k - 1, 0), 2 * (NZ - k))
            entry[i] = ((y - ty + NY) % NY * NC + (c + tc) % NC) * NZ + order
            return carry

        lax.fori_loop(0, per * nb, one, 0)

    own_rows = pl.ds(pl.multiple_of(x * quarter, quarter), quarter)

    def spread(it, s):
        for d in range(1, NX):
            theirs = pl.ds(pl.multiple_of(xs[d] * quarter, quarter), quarter)
            send(
                blocks[it].at[s, theirs],
                gath[it][0].at[x * per + s],
                x_send.at[it],
                x_recv.at[it],
                dev(dx=d),
            )
        gath[it][0][x * per + s] = blocks[it][s, own_rows, :]

    def singles_terms(it):
        if it == 0:
            local[3].wait()
        orbital = lax.broadcasted_iota(jnp.int32, (NOCC, width), 0)
        total = jnp.zeros((NOCC, width), jnp.float32)
        for s in range(per):
            row = lax.dot_general(
                jnp.broadcast_to(proj[s : s + 1, :], (8, width)),
                state[s],
                (((1,), (1,)), ((), ())),
                precision=HIGHEST,
                preferred_element_type=jnp.float32,
            )[0:1]
            row = jnp.broadcast_to(row, (NOCC, width))
            total += jnp.where(orbital == orbs[0, s], row, 0.0)
            total += jnp.where(orbital == orbs[1, s], row, 0.0)
        parts[it] = total

    for it in range(ITERS):
        g = gath[it]

        def push(k, h, k2, to, g=g, it=it):
            def part(j):
                return g[j].at[pl.ds(h * (group // 2), group // 2)]

            sent.append(send(part(k), part(k2), z_send.at[it], z_recv.at[it, k2 * 2 + h], to))

        def ready(k, h, g=g, it=it):
            arrived(g[k].at[pl.ds(h * (group // 2), group // 2)], z_recv.at[it, k * 2 + h])

        def deliver(ks, it=it, g=g):
            first, count = FIRST[ks[0]], len(ks)

            for i, (dx, dy, dc) in enumerate(steps):
                at = ((ys[dy] * NC + cs[dc]) * NX + xs[dx]) * per
                for j, k in enumerate(ks):
                    out_buf[it][i, first + j] = g[k][sel[k, at]]
            for j in range(count):
                recv[it][first + j, own_rows, :] = out_buf[it][0, first + j]
            for dx, dy, dc in far_first:
                i = steps.index((dx, dy, dc))
                if i:
                    send(
                        out_buf[it].at[i, pl.ds(first, count)],
                        recv[it].at[pl.ds((dy * NC + dc) * NZ + first, count), own_rows],
                        y_send.at[it],
                        y_recv.at[it],
                        dev(dx, dy, 0, dc),
                    )

        if it == 0:
            singles_terms(0)
            make_tables()
            pl.semaphore_wait(barrier, PLANE - 1 + NZ - 1)
            for s in range(per):
                spread(0, s)
        else:
            singles_terms(it)
        share = NOCC // NC
        mine = pl.ds(pl.multiple_of(c * share, share), share)
        other = pl.ds(pl.multiple_of((1 - c) * share, share), share)
        sent.append(send(parts.at[it, other], half.at[it], p_send.at[it, 0], p_recv.at[it, 0], dev(dc=1)))

        up, down = dev(dz=1), dev(dz=NZ - 1)
        arrived(g[0].at[pl.ds(0, group - per)], x_recv.at[it])
        for h in range(2):
            push(0, h, 1, up)
            push(0, h, 7, down)
        deliver((0,))

        arrived(half.at[it], p_recv.at[it, 0])
        sums[it, 0] = parts[it, mine, :] + half[it]
        for d in range(1, NY):
            sent.append(send(sums.at[it, 0], part_y.at[it, d - 1], p_send.at[it, 1], p_recv.at[it, 1], dev(dy=d)))

        for h in range(2):
            ready(1, h)
            push(1, h, 2, up)
            ready(7, h)
            push(7, h, 6, down)
        deliver((1, 7))

        arrived(part_y.at[it], p_recv.at[it, 1])
        sums[it, 1] = sums[it, 0] + part_y[it, 0] + part_y[it, 1] + part_y[it, 2]
        for d in range(1, NX):
            sent.append(send(sums.at[it, 1], part_x.at[it, d - 1], p_send.at[it, 2], p_recv.at[it, 2], dev(dx=d)))

        for h in range(2):
            ready(2, h)
            push(2, h, 3, up)
            ready(6, h)
            push(6, h, 5, down)
        deliver((2, 6))

        arrived(part_x.at[it], p_recv.at[it, 2])
        sums[it, 2] = sums[it, 1] + part_x[it, 0] + part_x[it, 1] + part_x[it, 2]
        for d in range(1, NZ):
            sent.append(send(sums.at[it, 2], part_z.at[it, d - 1], p_send.at[it, 3], p_recv.at[it, 3], dev(dz=d)))

        ready(3, 0)
        push(3, 0, 4, up)
        ready(5, 1)
        push(5, 1, 4, down)
        ready(5, 0)
        ready(3, 1)
        deliver((3, 5))
        ready(4, 0)
        ready(4, 1)
        deliver((4,))

        arrived(part_z.at[it], p_recv.at[it, 3])
        total = sums[it, 2]
        for i in range(NZ - 1):
            total += part_z[it, i]
        full[it, mine, :] = total
        sums[it, 3] = total
        sent.append(send(sums.at[it, 3], half.at[ITERS + it], p_send.at[it, 4], p_recv.at[it, 4], dev(dc=1)))

        if it == 0:
            make_entries()
            local[4].wait()
            local[5].wait()
            for s in range(per):
                e_row = ener[s : s + 1, :]
                den[s] = column(e_row) + e_row
                pcol[s] = column(proj[s : s + 1, :])
        if it == ITERS - 1:
            last_copy = pltpu.make_async_copy(state, last_hbm, local_sem.at[len(local) + 3])
            last_copy.start()
        else:
            for s in range(per):
                base[s] = integ[s].astype(jnp.float32) + den[s] * state[s]

        arrived(half.at[ITERS + it], p_recv.at[it, 4])
        full[it, other, :] = half[ITERS + it]
        if it == 0:
            local[6].wait()
        arrived(recv[it].at[pl.ds(0, (PLANE - 1) * NZ // NX)], y_recv.at[it])

        def one_slot(s, carry, it=it):
            acc = jnp.zeros((width, width), jnp.float32)
            scaled = [
                (
                    coup[s, k]
                    * jnp.dot(inter[s * nb + k], recv[it][entry[s * nb + k]], preferred_element_type=jnp.float32)
                ).astype(jnp.bfloat16)
                for k in range(nb)
            ]
            for k in range(0, nb, 2):
                acc += lax.dot_general(
                    jnp.concatenate(scaled[k : k + 2], axis=1),
                    jnp.concatenate([inter[s * nb + k], inter[s * nb + k + 1]], axis=1),
                    (((1,), (1,)), ((), ())),
                    preferred_element_type=jnp.float32,
                )
            left_row = full[it, pl.ds(orbs[0, s], 1), :]
            right_row = full[it, pl.ds(orbs[1, s], 1), :]
            added = column(left_row) * proj[pl.ds(s, 1), :] + pcol[s] * right_row - acc
            if it == ITERS - 1:
                change[s] = added
                pltpu.make_async_copy(change.at[s], change_hbm.at[s], local_sem.at[len(local) + 2]).start()
            else:
                new = state[s] - (base[s] + added) / den[s]
                state[s] = new
                blocks[it + 1][s] = new.astype(jnp.bfloat16)
                spread(it + 1, s)
            return carry

        lax.fori_loop(0, per, one_slot, 0)

    last_copy.wait()
    pltpu.make_async_copy(change, change_hbm, local_sem.at[len(local) + 2]).wait()
    for copy in sent:
        copy.wait_send()
    for it in range(ITERS):
        arrived(gath[it][0].at[pl.ds(0, group - per)], x_send.at[it])
        sends = recv[it].at[pl.ds(0, (PLANE - 1) * NZ // NX)]
        arrived(sends, y_send.at[it])


def body(amplitudes, integrals, energies, intersections, couplings, projector, pair_orbitals, coupled, pair_slot):
    per, width, _ = amplitudes.shape
    nb = coupled.shape[1]
    total = pair_slot.shape[0]
    group = NX * per
    quarter = width // NX
    bf16, f32, i32 = jnp.bfloat16, jnp.float32, jnp.int32
    smem = pl.BlockSpec(memory_space=pltpu.SMEM)
    hbm = pl.BlockSpec(memory_space=pltpu.HBM)
    dma = pltpu.SemaphoreType.DMA
    square = (per, width, width)
    share = NOCC // NC
    scratch = [pltpu.VMEM((group, quarter, width), bf16) for _ in range(2 * NZ)]
    scratch += [pltpu.VMEM((PLANE, NZ, quarter, width), bf16) for _ in range(2)]
    scratch += [pltpu.VMEM((NZ * NY * NC, width, width), bf16) for _ in range(2)]
    scratch += [pltpu.VMEM(square, bf16) for _ in range(2)]
    scratch += [
        pltpu.VMEM((ITERS, NOCC, width), f32),
        pltpu.VMEM((ITERS, NOCC, width), f32),
        pltpu.VMEM((2 * ITERS, share, width), f32),
        pltpu.VMEM((ITERS, NY - 1, share, width), f32),
        pltpu.VMEM((ITERS, NX - 1, share, width), f32),
        pltpu.VMEM((ITERS, NZ - 1, share, width), f32),
        pltpu.VMEM((ITERS, 4, share, width), f32),
        pltpu.VMEM((per * nb, width, width), bf16),
        pltpu.VMEM(square, bf16),
        pltpu.VMEM(square, f32),
        pltpu.VMEM((per, width), f32),
        pltpu.VMEM((per, width), f32),
        pltpu.VMEM((nb, total), i32),
        pltpu.VMEM((total // width, width), i32),
        pltpu.VMEM(square, f32),
        pltpu.VMEM(square, f32),
        pltpu.VMEM(square, f32),
        pltpu.VMEM(square, f32),
        pltpu.VMEM((NZ, width), i32),
        pltpu.VMEM((nb, width), i32),
        pltpu.SMEM((NZ, width), i32),
        pltpu.SMEM((nb, width), i32),
        pltpu.SMEM((per * nb,), i32),
        dma((11,)),
        dma((ITERS,)),
        dma((ITERS,)),
        dma((ITERS,)),
        dma((ITERS, 2 * NZ)),
        dma((ITERS,)),
        dma((ITERS,)),
        dma((ITERS, 5)),
        dma((ITERS, 5)),
    ]
    last, change = pl.pallas_call(
        kernel,
        out_shape=(
            jax.ShapeDtypeStruct(square, f32),
            jax.ShapeDtypeStruct(square, f32),
        ),
        in_specs=[smem, smem, smem, hbm, hbm, hbm, hbm, hbm, hbm, hbm],
        out_specs=(hbm, hbm),
        scratch_shapes=scratch,
        compiler_params=pltpu.CompilerParams(
            collective_id=0, has_side_effects=True, vmem_limit_bytes=67043328
        ),
    )(
        couplings,
        pair_orbitals.T,
        pair_slot,
        amplitudes,
        integrals,
        energies,
        intersections.reshape(per * nb, width, width),
        projector,
        coupled.T,
        pair_slot.reshape(total // width, width),
    )
    denom = energies[:, :, None] + energies[:, None, :]
    residual = integrals.astype(f32) + denom * last + change
    return (last - residual / denom, residual)


def solution(mesh):
    both = ("pairs", "orb")
    return jax.shard_map(
        body,
        mesh=mesh,
        in_specs=(
            P(both, None, None),
            P(both, None, None),
            P(both, None),
            P(both, None, None, None),
            P(both, None),
            P(both, None),
            P(both, None),
            P(),
            P(),
        ),
        out_specs=(P(both, None, None), P(both, None, None)),
        check_vma=False,
    )
```

```python
import jax
import jax.numpy as jnp
from jax import lax
from jax.experimental import pallas as pl
from jax.experimental.pallas import tpu as pltpu
from jax.sharding import PartitionSpec as P

ITERS = 2
NOCC = 32
NX, NY, NZ, NC = 4, 4, 8, 2
PLANE = NX * NY * NC
MESH = pl.DeviceIdType.MESH
HIGHEST = lax.Precision.HIGHEST
ROUNDS = ((0,), (1, 7), (2, 6), (3, 5), (4,))
FIRST = {0: 0, 1: 1, 2: 3, 3: 5, 4: 7}


def pair_index(y, z, c):
    return (y * NZ + z) * NC + c


def kernel(
    coup, orbs, slot_of, amp_hbm, integ_hbm, ener_hbm, inter_hbm, proj_hbm, coupled_hbm, slots_hbm, last_hbm, change_hbm,
    *scratch,
):
    gath = [scratch[0:NZ], scratch[NZ : 2 * NZ]]
    out_buf = scratch[2 * NZ : 2 * NZ + 2]
    recv = scratch[2 * NZ + 2 : 2 * NZ + 4]
    blocks = scratch[2 * NZ + 4 : 2 * NZ + 6]
    (parts, full, half, part_y, part_x, part_z, sums, inter, integ, state, ener, proj, cpl, slots, den, rden, pcol, base, change,
     sel_v, want_v, sel, want, entry,
     local_sem, x_send, x_recv, z_send, z_recv, y_send, y_recv, p_send, p_recv) = scratch[2 * NZ + 6 :]
    per, width, _ = state.shape
    nb = inter.shape[0] // per
    group = NX * per
    quarter = width // NX
    pair_idx = lax.axis_index("pairs")
    x = lax.axis_index("orb")
    y, z, c = pair_idx // (NZ * NC), pair_idx // NC % NZ, pair_idx % NC

    xs = [(x + d) % NX for d in range(NX)]
    ys = [(y + d) % NY for d in range(NY)]
    zs = [(z + d) % NZ for d in range(NZ)]
    cs = [(c + d) % NC for d in range(NC)]

    def dev(dx=0, dy=0, dz=0, dc=0):
        return (pair_index(ys[dy], zs[dz], cs[dc]), xs[dx])

    steps = [(dx, dy, dc) for dx in range(NX) for dy in range(NY) for dc in range(NC)]
    far_first = sorted(steps, key=lambda t: -(min(t[0], NX - t[0]) + min(t[1], NY - t[1])))

    local = [
        pltpu.make_async_copy(a, b, local_sem.at[i])
        for i, (a, b) in enumerate(
            (
                (amp_hbm, state),
                (coupled_hbm, cpl),
                (slots_hbm, slots),
                (proj_hbm, proj),
                (ener_hbm, ener),
                (integ_hbm, integ),
                (inter_hbm, inter),
            )
        )
    ]
    for copy in local:
        copy.start()

    barrier = pltpu.get_barrier_semaphore()

    up, down = dev(dz=1), dev(dz=NZ - 1)
    peers = [up, down] + [dev(dx, dy, 0, dc) for dx, dy, dc in far_first if (dx, dy, dc) != (0, 0, 0)]
    for peer in peers:
        pl.semaphore_signal(barrier, inc=1, device_id=peer, device_id_type=MESH)

    local[0].wait()
    for s in range(per):
        blocks[0][s] = state[s].astype(jnp.bfloat16)

    sent = []

    def send(src, dst, ssem, rsem, to):
        copy = pltpu.make_async_remote_copy(
            src_ref=src, dst_ref=dst, send_sem=ssem, recv_sem=rsem, device_id=to, device_id_type=MESH
        )
        copy.start()
        return copy

    def arrived(ref, sem):
        pltpu.make_async_copy(ref, ref, sem).wait()

    def column(row):
        return jnp.broadcast_to(row, (width, width)).T

    def make_tables():
        local[1].wait()
        local[2].wait()
        lane = lax.broadcasted_iota(jnp.int32, (nb, width), 1)
        span = width // NY
        wanted = jnp.zeros((nb, width), jnp.int32)
        for yy in range(NY):
            start = pl.multiple_of(yy * (NZ * span) + z // NY * width, width)
            tile = cpl[:, pl.ds(start, width)]
            tile = pltpu.roll(tile, (yy * span + width - z % NY * span) % width, 1)
            wanted = jnp.where(lane // span == yy, tile, wanted)
        want_v[...] = wanted
        row = lax.broadcasted_iota(jnp.int32, (width, width), 0)
        col = lax.broadcasted_iota(jnp.int32, (width, width), 1)
        slot = pair_index(y, (z + NZ - row // group) % NZ, c) * group + row % group
        held = jnp.zeros((width, width), jnp.int32)
        for r in range(slots.shape[0]):
            held += jnp.where(slots[r : r + 1, :] == slot, col + r * width, 0)
        shift = width // 2
        while shift:
            held += pltpu.roll(held, shift, 1)
            shift //= 2
        place = (row % group // per + NX - x) % NX * per + row % per
        hits = jnp.zeros((width, width), jnp.int32)
        for e in range(nb):
            hits = jnp.maximum(hits, jnp.where(wanted[e : e + 1, :] == held, place, 0))
        best = hits
        for r in range(1, per):
            best = jnp.maximum(best, pltpu.roll(hits, width - r, 1))
        sel_v[...] = jnp.max(best.reshape(NZ, group, width), axis=1)
        a = pltpu.make_async_copy(sel_v, sel, local_sem.at[len(local)])
        b = pltpu.make_async_copy(want_v, want, local_sem.at[len(local) + 1])
        a.start()
        b.start()
        a.wait()
        b.wait()

    def make_entries():
        mine = ((y * NC + c) * NX + x) * per

        def one(i, carry):
            t = slot_of[want[i % nb, mine + i // nb]] // group
            ty, tz, tc = t // (NZ * NC), t // NC % NZ, t % NC
            k = (z - tz + NZ) % NZ
            order = jnp.where(k <= NZ // 2, jnp.maximum(2 * k - 1, 0), 2 * (NZ - k))
            entry[i] = ((y - ty + NY) % NY * NC + (c + tc) % NC) * NZ + order
            return carry

        lax.fori_loop(0, per * nb, one, 0)

    own_rows = pl.ds(pl.multiple_of(x * quarter, quarter), quarter)

    def spread(it, s):
        gath[it][0][s] = blocks[it][s, own_rows, :]
        for d in (1, 3, 2):
            theirs = pl.ds(pl.multiple_of(xs[d] * quarter, quarter), quarter)
            send(
                blocks[it].at[s, theirs],
                gath[it][0].at[(NX - d) * per + s],
                x_send.at[it],
                x_recv.at[it, NX - d],
                dev(dx=d),
            )

    def singles_terms(it):
        if it == 0:
            local[3].wait()
        orbital = lax.broadcasted_iota(jnp.int32, (NOCC, width), 0)
        total = jnp.zeros((NOCC, width), jnp.float32)
        for s in range(per):
            row = lax.dot_general(
                jnp.broadcast_to(proj[s : s + 1, :], (8, width)),
                state[s],
                (((1,), (1,)), ((), ())),
                precision=HIGHEST,
                preferred_element_type=jnp.float32,
            )[0:1]
            row = jnp.broadcast_to(row, (NOCC, width))
            total += jnp.where(orbital == orbs[0, s], row, 0.0)
            total += jnp.where(orbital == orbs[1, s], row, 0.0)
        parts[it] = total

    for it in range(ITERS):
        g = gath[it]

        def piece(k, q, g=g):
            return g[k].at[pl.ds(q * per, per)]

        def push(k, q, k2, to, piece=piece, it=it):
            sent.append(send(piece(k, q), piece(k2, q), z_send.at[it], z_recv.at[it, k2 * NX + q], to))

        def ready(k, q, piece=piece, it=it):
            arrived(piece(k, q), z_recv.at[it, k * NX + q])

        def ring(k, k2, to, it=it):
            sent.append(
                send(part_z.at[it, k], part_z.at[it, k2], p_send.at[it, 3], p_recv.at[it, 3 + k2], to)
            )

        def ringed(k, it=it):
            arrived(part_z.at[it, k], p_recv.at[it, 3 + k])

        def deliver(ks, it=it, g=g):
            first, count = FIRST[ks[0]], len(ks)

            for i, (dx, dy, dc) in enumerate(steps):
                at = ((ys[dy] * NC + cs[dc]) * NX + xs[dx]) * per
                for j, k in enumerate(ks):
                    out_buf[it][i, first + j] = g[k][sel[k, at]]
            for j in range(count):
                recv[it][first + j, own_rows, :] = out_buf[it][0, first + j]
            for dx, dy, dc in far_first:
                i = steps.index((dx, dy, dc))
                if i:
                    send(
                        out_buf[it].at[i, pl.ds(first, count)],
                        recv[it].at[pl.ds((dy * NC + dc) * NZ + first, count), own_rows],
                        y_send.at[it],
                        y_recv.at[it],
                        dev(dx, dy, 0, dc),
                    )

        if it == 0:
            singles_terms(0)
            make_tables()
            pl.semaphore_wait(barrier, len(peers))
            for s in range(per):
                spread(0, s)
        push(0, 0, 1, up)
        push(0, 0, 7, down)
        if it:
            singles_terms(it)
        share = NOCC // NC
        mine = pl.ds(pl.multiple_of(c * share, share), share)
        other = pl.ds(pl.multiple_of((1 - c) * share, share), share)
        sent.append(send(parts.at[it, other], half.at[it], p_send.at[it, 0], p_recv.at[it, 0], dev(dc=1)))

        for q in (1, 3, 2):
            arrived(piece(0, q), x_recv.at[it, q])
            push(0, q, 1, up)
            push(0, q, 7, down)
        arrived(half.at[it], p_recv.at[it, 0])
        sums[it, 0] = parts[it, mine, :] + half[it]
        for d in range(1, NY):
            sent.append(send(sums.at[it, 0], part_y.at[it, d - 1], p_send.at[it, 1], p_recv.at[it, 1], dev(dy=d)))
        deliver((0,))

        for q in (0, 1, 3, 2):
            ready(1, q)
            push(1, q, 2, up)
            ready(7, q)
            push(7, q, 6, down)
        arrived(part_y.at[it], p_recv.at[it, 1])
        sums[it, 1] = sums[it, 0] + part_y[it, 0] + part_y[it, 1] + part_y[it, 2]
        for d in range(1, NX):
            sent.append(send(sums.at[it, 1], part_x.at[it, d - 1], p_send.at[it, 2], p_recv.at[it, 2], dev(dx=d)))
        deliver((1, 7))

        for q in (0, 1, 3, 2):
            ready(2, q)
            push(2, q, 3, up)
            ready(6, q)
            push(6, q, 5, down)
        arrived(part_x.at[it], p_recv.at[it, 2])
        part_z[it, 0] = sums[it, 1] + part_x[it, 0] + part_x[it, 1] + part_x[it, 2]
        ring(0, 1, up)
        ring(0, 7, down)
        deliver((2, 6))

        for q in (0, 1, 3, 2):
            ready(3, q)
            if q in (0, 1):
                push(3, q, 4, up)
            ready(5, q)
            if q in (2, 3):
                push(5, q, 4, down)
        ringed(1)
        ring(1, 2, up)
        ringed(7)
        ring(7, 6, down)
        deliver((3, 5))
        for q in (0, 1, 3, 2):
            ready(4, q)
        deliver((4,))

        ringed(2)
        ring(2, 3, up)
        ringed(6)
        ring(6, 5, down)
        if it == 0:
            make_entries()
            local[4].wait()
            for s in range(per):
                e_row = ener[s : s + 1, :]
                den[s] = column(e_row) + e_row
                rden[s] = 1.0 / den[s]
                pcol[s] = column(proj[s : s + 1, :])
            local[5].wait()
        ringed(3)
        ring(3, 4, up)
        ringed(5)
        ringed(4)
        total = part_z[it, 0]
        for k in range(1, NZ):
            total += part_z[it, k]
        full[it, mine, :] = total
        sums[it, 2] = total
        sent.append(send(sums.at[it, 2], half.at[ITERS + it], p_send.at[it, 4], p_recv.at[it, 2 * NX + 3], dev(dc=1)))
        arrived(half.at[ITERS + it], p_recv.at[it, 2 * NX + 3])
        full[it, other, :] = half[ITERS + it]
        if it == ITERS - 1:
            last_copy = pltpu.make_async_copy(state, last_hbm, local_sem.at[len(local) + 3])
            last_copy.start()
        for s in range(per):
            left_row = full[it, pl.ds(orbs[0, s], 1), :]
            right_row = full[it, pl.ds(orbs[1, s], 1), :]
            base[s] = column(left_row) * proj[s : s + 1, :] + pcol[s] * right_row
            if it < ITERS - 1:
                whole = integ[s].astype(jnp.float32) + den[s] * state[s] + base[s]
                base[s] = state[s] - whole / den[s]
        if it == 0:
            local[6].wait()
        arrived(recv[it].at[pl.ds(0, (PLANE - 1) * NZ // NX)], y_recv.at[it])

        def one_slot(s, carry, it=it):
            acc = jnp.zeros((width, width), jnp.float32)
            scaled = [
                (
                    coup[s, k]
                    * jnp.dot(inter[s * nb + k], recv[it][entry[s * nb + k]], preferred_element_type=jnp.float32)
                ).astype(jnp.bfloat16)
                for k in range(nb)
            ]
            for k in range(0, nb, 2):
                acc += lax.dot_general(
                    jnp.concatenate(scaled[k : k + 2], axis=1),
                    jnp.concatenate([inter[s * nb + k], inter[s * nb + k + 1]], axis=1),
                    (((1,), (1,)), ((), ())),
                    preferred_element_type=jnp.float32,
                )
            if it == ITERS - 1:
                change[s] = base[s] - acc
                pltpu.make_async_copy(change.at[s], change_hbm.at[s], local_sem.at[len(local) + 2]).start()
            else:
                new = base[s] + acc * rden[s]
                state[s] = new
                blocks[it + 1][s] = new.astype(jnp.bfloat16)
                spread(it + 1, s)
            return carry

        lax.fori_loop(0, per, one_slot, 0)

    last_copy.wait()
    pltpu.make_async_copy(change, change_hbm, local_sem.at[len(local) + 2]).wait()
    for copy in sent:
        copy.wait_send()
    for it in range(ITERS):
        arrived(gath[it][0].at[pl.ds(0, group - per)], x_send.at[it])
        sends = recv[it].at[pl.ds(0, (PLANE - 1) * NZ // NX)]
        arrived(sends, y_send.at[it])


def body(amplitudes, integrals, energies, intersections, couplings, projector, pair_orbitals, coupled, pair_slot):
    per, width, _ = amplitudes.shape
    nb = coupled.shape[1]
    total = pair_slot.shape[0]
    group = NX * per
    quarter = width // NX
    bf16, f32, i32 = jnp.bfloat16, jnp.float32, jnp.int32
    smem = pl.BlockSpec(memory_space=pltpu.SMEM)
    hbm = pl.BlockSpec(memory_space=pltpu.HBM)
    dma = pltpu.SemaphoreType.DMA
    square = (per, width, width)
    share = NOCC // NC
    scratch = [pltpu.VMEM((group, quarter, width), bf16) for _ in range(2 * NZ)]
    scratch += [pltpu.VMEM((PLANE, NZ, quarter, width), bf16) for _ in range(2)]
    scratch += [pltpu.VMEM((NZ * NY * NC, width, width), bf16) for _ in range(2)]
    scratch += [pltpu.VMEM(square, bf16) for _ in range(2)]
    scratch += [
        pltpu.VMEM((ITERS, NOCC, width), f32),
        pltpu.VMEM((ITERS, NOCC, width), f32),
        pltpu.VMEM((2 * ITERS, share, width), f32),
        pltpu.VMEM((ITERS, NY - 1, share, width), f32),
        pltpu.VMEM((ITERS, NX - 1, share, width), f32),
        pltpu.VMEM((ITERS, NZ, share, width), f32),
        pltpu.VMEM((ITERS, 4, share, width), f32),
        pltpu.VMEM((per * nb, width, width), bf16),
        pltpu.VMEM(square, bf16),
        pltpu.VMEM(square, f32),
        pltpu.VMEM((per, width), f32),
        pltpu.VMEM((per, width), f32),
        pltpu.VMEM((nb, total), i32),
        pltpu.VMEM((total // width, width), i32),
        pltpu.VMEM(square, f32),
        pltpu.VMEM(square, f32),
        pltpu.VMEM(square, f32),
        pltpu.VMEM(square, f32),
        pltpu.VMEM(square, f32),
        pltpu.VMEM((NZ, width), i32),
        pltpu.VMEM((nb, width), i32),
        pltpu.SMEM((NZ, width), i32),
        pltpu.SMEM((nb, width), i32),
        pltpu.SMEM((per * nb,), i32),
        dma((11,)),
        dma((ITERS,)),
        dma((ITERS, NX)),
        dma((ITERS,)),
        dma((ITERS, NX * NZ)),
        dma((ITERS,)),
        dma((ITERS,)),
        dma((ITERS, 5)),
        dma((ITERS, NZ + 4)),
    ]
    last, change = pl.pallas_call(
        kernel,
        out_shape=(
            jax.ShapeDtypeStruct(square, f32),
            jax.ShapeDtypeStruct(square, f32),
        ),
        in_specs=[smem, smem, smem, hbm, hbm, hbm, hbm, hbm, hbm, hbm],
        out_specs=(hbm, hbm),
        scratch_shapes=scratch,
        compiler_params=pltpu.CompilerParams(
            collective_id=0, has_side_effects=True, vmem_limit_bytes=67043328
        ),
    )(
        couplings,
        pair_orbitals.T,
        pair_slot,
        amplitudes,
        integrals,
        energies,
        intersections.reshape(per * nb, width, width),
        projector,
        coupled.T,
        pair_slot.reshape(total // width, width),
    )
    denom = energies[:, :, None] + energies[:, None, :]
    residual = integrals.astype(f32) + denom * last + change
    return (last - residual / denom, residual)


def solution(mesh):
    both = ("pairs", "orb")
    return jax.shard_map(
        body,
        mesh=mesh,
        in_specs=(
            P(both, None, None),
            P(both, None, None),
            P(both, None),
            P(both, None, None, None),
            P(both, None),
            P(both, None),
            P(both, None),
            P(),
            P(),
        ),
        out_specs=(P(both, None, None), P(both, None, None)),
        check_vma=False,
    )
```

```python
import jax
import jax.numpy as jnp
from jax import lax
from jax.experimental import pallas as pl
from jax.experimental.pallas import tpu as pltpu
from jax.sharding import PartitionSpec as P

ITERS = 2
NOCC = 32
NX, NY, NZ, NC = 4, 4, 8, 2
PLANE = NX * NY * NC
MESH = pl.DeviceIdType.MESH
HIGHEST = lax.Precision.HIGHEST
ROUNDS = ((0,), (1, 7), (2, 6), (3, 5, 4))
FIRST = {0: 0, 1: 1, 2: 3, 3: 5}


def pair_index(y, z, c):
    return (y * NZ + z) * NC + c


def kernel(
    coup, orbs, slot_of, amp_hbm, integ_hbm, ener_hbm, inter_hbm, proj_hbm, coupled_hbm, slots_hbm, last_hbm, change_hbm,
    *scratch,
):
    gath = [scratch[0:NZ], scratch[NZ : 2 * NZ]]
    out_buf = scratch[2 * NZ : 2 * NZ + 2]
    recv = scratch[2 * NZ + 2 : 2 * NZ + 4]
    blocks = scratch[2 * NZ + 4 : 2 * NZ + 6]
    (parts, full, half, part_y, part_x, part_z, sums, inter, integ, state, ener, proj, cpl, slots, den, rden, pcol, base, change,
     sel_v, want_v, sel, want, entry,
     local_sem, x_send, z_send, z_recv, y_send, y_recv, p_send, p_recv) = scratch[2 * NZ + 6 :]
    per, width, _ = state.shape
    nb = inter.shape[0] // per
    group = NX * per
    quarter = width // NX
    pair_idx = lax.axis_index("pairs")
    x = lax.axis_index("orb")
    y, z, c = pair_idx // (NZ * NC), pair_idx // NC % NZ, pair_idx % NC

    xs = [(x + d) % NX for d in range(NX)]
    ys = [(y + d) % NY for d in range(NY)]
    zs = [(z + d) % NZ for d in range(NZ)]
    cs = [(c + d) % NC for d in range(NC)]

    def dev(dx=0, dy=0, dz=0, dc=0):
        return (pair_index(ys[dy], zs[dz], cs[dc]), xs[dx])

    steps = [(dx, dy, dc) for dx in range(NX) for dy in range(NY) for dc in range(NC)]
    far_first = sorted(steps, key=lambda t: -(min(t[0], NX - t[0]) + min(t[1], NY - t[1])))

    local = [
        pltpu.make_async_copy(a, b, local_sem.at[i])
        for i, (a, b) in enumerate(
            (
                (amp_hbm, state),
                (coupled_hbm, cpl),
                (slots_hbm, slots),
                (proj_hbm, proj),
                (ener_hbm, ener),
                (integ_hbm, integ),
                (inter_hbm, inter),
            )
        )
    ]
    for copy in local:
        copy.start()

    barrier = pltpu.get_barrier_semaphore()

    up, down = dev(dz=1), dev(dz=NZ - 1)
    peers = [up, down]
    peers += [dev(dx, dy, 0, dc) for dx, dy, dc in far_first if (dx, dy, dc) != (0, 0, 0)]
    for peer in peers:
        pl.semaphore_signal(barrier, inc=1, device_id=peer, device_id_type=MESH)

    local[0].wait()
    for s in range(per):
        blocks[0][s] = state[s].astype(jnp.bfloat16)

    sent = []

    def send(src, dst, ssem, rsem, to):
        copy = pltpu.make_async_remote_copy(
            src_ref=src, dst_ref=dst, send_sem=ssem, recv_sem=rsem, device_id=to, device_id_type=MESH
        )
        copy.start()
        return copy

    def arrived(ref, sem):
        pltpu.make_async_copy(ref, ref, sem).wait()

    def column(row):
        return jnp.broadcast_to(row, (width, width)).T

    def make_tables():
        local[1].wait()
        local[2].wait()
        lane = lax.broadcasted_iota(jnp.int32, (nb, width), 1)
        span = width // NY
        wanted = jnp.zeros((nb, width), jnp.int32)
        for yy in range(NY):
            start = pl.multiple_of(yy * (NZ * span) + z // NY * width, width)
            tile = cpl[:, pl.ds(start, width)]
            tile = pltpu.roll(tile, (yy * span + width - z % NY * span) % width, 1)
            wanted = jnp.where(lane // span == yy, tile, wanted)
        want_v[...] = wanted
        row = lax.broadcasted_iota(jnp.int32, (width, width), 0)
        col = lax.broadcasted_iota(jnp.int32, (width, width), 1)
        slot = pair_index(y, (z + NZ - row // group) % NZ, c) * group + row % group
        held = jnp.zeros((width, width), jnp.int32)
        for r in range(slots.shape[0]):
            held += jnp.where(slots[r : r + 1, :] == slot, col + r * width, 0)
        shift = width // 2
        while shift:
            held += pltpu.roll(held, shift, 1)
            shift //= 2
        place = (row % group // per + NX - x) % NX * per + row % per
        hits = jnp.zeros((width, width), jnp.int32)
        for e in range(nb):
            hits = jnp.maximum(hits, jnp.where(wanted[e : e + 1, :] == held, place, 0))
        best = hits
        for r in range(1, per):
            best = jnp.maximum(best, pltpu.roll(hits, width - r, 1))
        sel_v[...] = jnp.max(best.reshape(NZ, group, width), axis=1)
        a = pltpu.make_async_copy(sel_v, sel, local_sem.at[len(local)])
        b = pltpu.make_async_copy(want_v, want, local_sem.at[len(local) + 1])
        a.start()
        b.start()
        a.wait()
        b.wait()

    def make_entries():
        mine = ((y * NC + c) * NX + x) * per

        def one(i, carry):
            t = slot_of[want[i % nb, mine + i // nb]] // group
            ty, tz, tc = t // (NZ * NC), t // NC % NZ, t % NC
            k = (z - tz + NZ) % NZ
            order = jnp.where(k <= NZ // 2, jnp.maximum(2 * k - 1, 0), 2 * (NZ - k))
            entry[i] = ((y - ty + NY) % NY * NC + (c + tc) % NC) * NZ + order
            return carry

        lax.fori_loop(0, per * nb, one, 0)

    own_rows = pl.ds(pl.multiple_of(x * quarter, quarter), quarter)

    def spread(it, s, count=1):
        slots_in = pl.ds(s, count)
        for d in (1, 3, 2):
            theirs = pl.ds(pl.multiple_of(xs[d] * quarter, quarter), quarter)
            send(
                blocks[it].at[slots_in, theirs],
                gath[it][0].at[pl.ds((NX - d) * per + s, count)],
                x_send.at[it],
                z_recv.at[it, NX - d],
                dev(dx=d),
            )
        gath[it][0][slots_in] = blocks[it][slots_in, own_rows, :]

    def singles_terms(it):
        if it == 0:
            local[3].wait()
        orbital = lax.broadcasted_iota(jnp.int32, (NOCC, width), 0)
        total = jnp.zeros((NOCC, width), jnp.float32)
        for s in range(per):
            row = lax.dot_general(
                jnp.broadcast_to(proj[s : s + 1, :], (8, width)),
                state[s],
                (((1,), (1,)), ((), ())),
                precision=HIGHEST,
                preferred_element_type=jnp.float32,
            )[0:1]
            row = jnp.broadcast_to(row, (NOCC, width))
            total += jnp.where(orbital == orbs[0, s], row, 0.0)
            total += jnp.where(orbital == orbs[1, s], row, 0.0)
        parts[it] = total

    for it in range(ITERS):
        g = gath[it]

        def piece(k, q, g=g):
            return g[k].at[pl.ds(q * per, per)]

        def push(k, q, k2, to, piece=piece, it=it):
            sent.append(send(piece(k, q), piece(k2, q), z_send.at[it], z_recv.at[it, k2 * NX + q], to))

        def ready(k, q, piece=piece, it=it):
            arrived(piece(k, q), z_recv.at[it, k * NX + q])

        def ring(k, k2, to, it=it):
            sent.append(
                send(part_z.at[it, k], part_z.at[it, k2], p_send.at[it, 3], p_recv.at[it, 3 + k2], to)
            )

        def ringed(k, it=it):
            arrived(part_z.at[it, k], p_recv.at[it, 3 + k])

        def deliver(ks, it=it, g=g):
            first, count = FIRST[ks[0]], len(ks)

            for i, (dx, dy, dc) in enumerate(steps):
                at = ((ys[dy] * NC + cs[dc]) * NX + xs[dx]) * per
                for j, k in enumerate(ks):
                    out_buf[it][i, first + j] = g[k][sel[k, at]]
            for j in range(count):
                recv[it][first + j, own_rows, :] = out_buf[it][0, first + j]
            for dx, dy, dc in far_first:
                i = steps.index((dx, dy, dc))
                if i:
                    send(
                        out_buf[it].at[i, pl.ds(first, count)],
                        recv[it].at[pl.ds((dy * NC + dc) * NZ + first, count), own_rows],
                        y_send.at[it],
                        y_recv.at[it],
                        dev(dx, dy, 0, dc),
                    )

        if it == 0:
            singles_terms(0)
            make_tables()
            pl.semaphore_wait(barrier, len(peers))
            spread(0, 0, per)
        push(0, 0, 1, up)
        push(0, 0, 7, down)
        if it:
            singles_terms(it)
        share = NOCC // NC
        mine = pl.ds(pl.multiple_of(c * share, share), share)
        other = pl.ds(pl.multiple_of((1 - c) * share, share), share)
        sent.append(send(parts.at[it, other], half.at[it], p_send.at[it, 0], p_recv.at[it, 0], dev(dc=1)))

        for q in (1, 3, 2):
            ready(0, q)
            push(0, q, 1, up)
            push(0, q, 7, down)
        arrived(half.at[it], p_recv.at[it, 0])
        sums[it, 0] = parts[it, mine, :] + half[it]
        for d in range(1, NY):
            sent.append(send(sums.at[it, 0], part_y.at[it, d - 1], p_send.at[it, 1], p_recv.at[it, 1], dev(dy=d)))
        deliver((0,))

        for q in (0, 1, 3, 2):
            ready(1, q)
            push(1, q, 2, up)
            ready(7, q)
            push(7, q, 6, down)
        arrived(part_y.at[it], p_recv.at[it, 1])
        sums[it, 1] = sums[it, 0] + part_y[it, 0] + part_y[it, 1] + part_y[it, 2]
        for d in range(1, NX):
            sent.append(send(sums.at[it, 1], part_x.at[it, d - 1], p_send.at[it, 2], p_recv.at[it, 2], dev(dx=d)))
        deliver((1, 7))

        for q in (0, 1, 3, 2):
            ready(2, q)
            push(2, q, 3, up)
            ready(6, q)
            push(6, q, 5, down)
        arrived(part_x.at[it], p_recv.at[it, 2])
        part_z[it, 0] = sums[it, 1] + part_x[it, 0] + part_x[it, 1] + part_x[it, 2]
        ring(0, 1, up)
        ring(0, 7, down)
        deliver((2, 6))

        for q in (0, 1, 3, 2):
            ready(3, q)
            if q in (0, 1):
                push(3, q, 4, up)
            ready(5, q)
            if q in (2, 3):
                push(5, q, 4, down)
        ringed(1)
        ring(1, 2, up)
        ringed(7)
        ring(7, 6, down)
        for q in (0, 1, 3, 2):
            ready(4, q)
        deliver((3, 5, 4))

        ringed(2)
        ring(2, 3, up)
        ringed(6)
        ring(6, 5, down)
        if it == 0:
            make_entries()
            local[4].wait()
            for s in range(per):
                e_row = ener[s : s + 1, :]
                den[s] = column(e_row) + e_row
                rden[s] = 1.0 / den[s]
                pcol[s] = column(proj[s : s + 1, :])
            local[5].wait()
        ringed(3)
        ring(3, 4, up)
        ringed(5)
        ringed(4)
        total = part_z[it, 0]
        for k in range(1, NZ):
            total += part_z[it, k]
        full[it, mine, :] = total
        sums[it, 2] = total
        sent.append(send(sums.at[it, 2], half.at[ITERS + it], p_send.at[it, 4], p_recv.at[it, 2 * NX + 3], dev(dc=1)))
        arrived(half.at[ITERS + it], p_recv.at[it, 2 * NX + 3])
        full[it, other, :] = half[ITERS + it]
        if it == ITERS - 1:
            last_copy = pltpu.make_async_copy(state, last_hbm, local_sem.at[len(local) + 3])
            last_copy.start()
        for s in range(per):
            left_row = full[it, pl.ds(orbs[0, s], 1), :]
            right_row = full[it, pl.ds(orbs[1, s], 1), :]
            base[s] = column(left_row) * proj[s : s + 1, :] + pcol[s] * right_row
            if it < ITERS - 1:
                whole = integ[s].astype(jnp.float32) + den[s] * state[s] + base[s]
                base[s] = state[s] - whole / den[s]
        if it == 0:
            local[6].wait()
        arrived(recv[it].at[pl.ds(0, (PLANE - 1) * NZ // NX)], y_recv.at[it])

        def one_slot(s, it=it):
            acc = jnp.zeros((width, width), jnp.float32)
            scaled = [
                (
                    coup[s, k]
                    * jnp.dot(inter[s * nb + k], recv[it][entry[s * nb + k]], preferred_element_type=jnp.float32)
                ).astype(jnp.bfloat16)
                for k in range(nb)
            ]
            for k in range(0, nb, 2):
                acc += lax.dot_general(
                    jnp.concatenate(scaled[k : k + 2], axis=1),
                    jnp.concatenate([inter[s * nb + k], inter[s * nb + k + 1]], axis=1),
                    (((1,), (1,)), ((), ())),
                    preferred_element_type=jnp.float32,
                )
            if it == ITERS - 1:
                change[s] = base[s] - acc
                pltpu.make_async_copy(change.at[s], change_hbm.at[s], local_sem.at[len(local) + 2]).start()
            else:
                new = base[s] + acc * rden[s]
                state[s] = new
                blocks[it + 1][s] = new.astype(jnp.bfloat16)
                spread(it + 1, s)

        for s in range(per):
            one_slot(s)

    last_copy.wait()
    pltpu.make_async_copy(change, change_hbm, local_sem.at[len(local) + 2]).wait()
    for copy in sent:
        copy.wait_send()
    for it in range(ITERS):
        arrived(gath[it][0].at[pl.ds(0, group - per)], x_send.at[it])
        sends = recv[it].at[pl.ds(0, (PLANE - 1) * NZ // NX)]
        arrived(sends, y_send.at[it])


def body(amplitudes, integrals, energies, intersections, couplings, projector, pair_orbitals, coupled, pair_slot):
    per, width, _ = amplitudes.shape
    nb = coupled.shape[1]
    total = pair_slot.shape[0]
    group = NX * per
    quarter = width // NX
    bf16, f32, i32 = jnp.bfloat16, jnp.float32, jnp.int32
    smem = pl.BlockSpec(memory_space=pltpu.SMEM)
    hbm = pl.BlockSpec(memory_space=pltpu.HBM)
    dma = pltpu.SemaphoreType.DMA
    square = (per, width, width)
    share = NOCC // NC
    scratch = [pltpu.VMEM((group, quarter, width), bf16) for _ in range(2 * NZ)]
    scratch += [pltpu.VMEM((PLANE, NZ, quarter, width), bf16) for _ in range(2)]
    scratch += [pltpu.VMEM((NZ * NY * NC, width, width), bf16) for _ in range(2)]
    scratch += [pltpu.VMEM(square, bf16) for _ in range(2)]
    scratch += [
        pltpu.VMEM((ITERS, NOCC, width), f32),
        pltpu.VMEM((ITERS, NOCC, width), f32),
        pltpu.VMEM((2 * ITERS, share, width), f32),
        pltpu.VMEM((ITERS, NY - 1, share, width), f32),
        pltpu.VMEM((ITERS, NX - 1, share, width), f32),
        pltpu.VMEM((ITERS, NZ, share, width), f32),
        pltpu.VMEM((ITERS, 4, share, width), f32),
        pltpu.VMEM((per * nb, width, width), bf16),
        pltpu.VMEM(square, bf16),
        pltpu.VMEM(square, f32),
        pltpu.VMEM((per, width), f32),
        pltpu.VMEM((per, width), f32),
        pltpu.VMEM((nb, total), i32),
        pltpu.VMEM((total // width, width), i32),
        pltpu.VMEM(square, f32),
        pltpu.VMEM(square, f32),
        pltpu.VMEM(square, f32),
        pltpu.VMEM(square, f32),
        pltpu.VMEM(square, f32),
        pltpu.VMEM((NZ, width), i32),
        pltpu.VMEM((nb, width), i32),
        pltpu.SMEM((NZ, width), i32),
        pltpu.SMEM((nb, width), i32),
        pltpu.SMEM((per * nb,), i32),
        dma((11,)),
        dma((ITERS,)),
        dma((ITERS,)),
        dma((ITERS, NX * NZ)),
        dma((ITERS,)),
        dma((ITERS,)),
        dma((ITERS, 5)),
        dma((ITERS, NZ + 4)),
    ]
    last, change = pl.pallas_call(
        kernel,
        out_shape=(
            jax.ShapeDtypeStruct(square, f32),
            jax.ShapeDtypeStruct(square, f32),
        ),
        in_specs=[smem, smem, smem, hbm, hbm, hbm, hbm, hbm, hbm, hbm],
        out_specs=(hbm, hbm),
        scratch_shapes=scratch,
        compiler_params=pltpu.CompilerParams(
            collective_id=0, has_side_effects=True, vmem_limit_bytes=67043328
        ),
    )(
        couplings,
        pair_orbitals.T,
        pair_slot,
        amplitudes,
        integrals,
        energies,
        intersections.reshape(per * nb, width, width),
        projector,
        coupled.T,
        pair_slot.reshape(total // width, width),
    )
    denom = energies[:, :, None] + energies[:, None, :]
    residual = integrals.astype(f32) + denom * last + change
    return (last - residual / denom, residual)


def solution(mesh):
    both = ("pairs", "orb")
    return jax.shard_map(
        body,
        mesh=mesh,
        in_specs=(
            P(both, None, None),
            P(both, None, None),
            P(both, None),
            P(both, None, None, None),
            P(both, None),
            P(both, None),
            P(both, None),
            P(),
            P(),
        ),
        out_specs=(P(both, None, None), P(both, None, None)),
        check_vma=False,
    )
```

```python
import jax
import jax.numpy as jnp
from jax import lax
from jax.experimental import pallas as pl
from jax.experimental.pallas import tpu as pltpu
from jax.sharding import PartitionSpec as P

ITERS = 2
NOCC = 32
NX, NY, NZ, NC = 4, 4, 8, 2
PLANE = NX * NY * NC
MESH = pl.DeviceIdType.MESH
HIGHEST = lax.Precision.HIGHEST
ROUNDS = ((0,), (1, 7), (2, 6), (3, 5, 4))
FIRST = {0: 0, 1: 1, 2: 3, 3: 5}


def pair_index(y, z, c):
    return (y * NZ + z) * NC + c


def kernel(
    coup_hbm, orbs_hbm, slot_hbm, amp_hbm, integ_hbm, ener_hbm, inter_hbm, proj_hbm, coupled_hbm, slots_hbm, last_hbm, change_hbm,
    *scratch,
):
    gath = [scratch[0:NZ], scratch[NZ : 2 * NZ]]
    out_buf = scratch[2 * NZ : 2 * NZ + 2]
    recv = scratch[2 * NZ + 2 : 2 * NZ + 4]
    blocks = scratch[2 * NZ + 4 : 2 * NZ + 6]
    (parts, full, half, part_y, part_x, part_z, sums, inter, integ, state, ener, proj, cpl, slots, den, rden, pcol, base, change,
     sel_v, want_v, sel, want, entry, coup, orbs, slot_of,
     local_sem, x_send, z_send, z_recv, y_send, y_recv, p_send, p_recv) = scratch[2 * NZ + 6 :]
    per, width, _ = state.shape
    nb = inter.shape[0] // per
    group = NX * per
    quarter = width // NX
    pair_idx = lax.axis_index("pairs")
    x = lax.axis_index("orb")
    y, z, c = pair_idx // (NZ * NC), pair_idx // NC % NZ, pair_idx % NC

    xs = [(x + d) % NX for d in range(NX)]
    ys = [(y + d) % NY for d in range(NY)]
    zs = [(z + d) % NZ for d in range(NZ)]
    cs = [(c + d) % NC for d in range(NC)]

    def dev(dx=0, dy=0, dz=0, dc=0):
        return (pair_index(ys[dy], zs[dz], cs[dc]), xs[dx])

    steps = [(dx, dy, dc) for dx in range(NX) for dy in range(NY) for dc in range(NC)]
    far_first = sorted(steps, key=lambda t: -(min(t[0], NX - t[0]) + min(t[1], NY - t[1])))

    local = [
        pltpu.make_async_copy(a, b, local_sem.at[i])
        for i, (a, b) in enumerate(
            (
                (amp_hbm, state),
                (coupled_hbm, cpl),
                (slots_hbm, slots),
                (proj_hbm, proj),
                (ener_hbm, ener),
                (integ_hbm, integ),
                (inter_hbm, inter),
                (orbs_hbm, orbs),
                (slot_hbm, slot_of),
                (coup_hbm, coup),
            )
        )
    ]
    for copy in local:
        copy.start()

    barrier = pltpu.get_barrier_semaphore()

    up, down = dev(dz=1), dev(dz=NZ - 1)
    peers = [up, down]
    peers += [dev(dx, dy, 0, dc) for dx, dy, dc in far_first if (dx, dy, dc) != (0, 0, 0)]
    for peer in peers:
        pl.semaphore_signal(barrier, inc=1, device_id=peer, device_id_type=MESH)

    local[0].wait()
    for s in range(per):
        blocks[0][s] = state[s].astype(jnp.bfloat16)

    sent = []

    def send(src, dst, ssem, rsem, to):
        copy = pltpu.make_async_remote_copy(
            src_ref=src, dst_ref=dst, send_sem=ssem, recv_sem=rsem, device_id=to, device_id_type=MESH
        )
        copy.start()
        return copy

    def arrived(ref, sem):
        pltpu.make_async_copy(ref, ref, sem).wait()

    def column(row):
        return jnp.broadcast_to(row, (width, width)).T

    def make_tables():
        local[1].wait()
        local[2].wait()
        lane = lax.broadcasted_iota(jnp.int32, (nb, width), 1)
        span = width // NY
        wanted = jnp.zeros((nb, width), jnp.int32)
        for yy in range(NY):
            start = pl.multiple_of(yy * (NZ * span) + z // NY * width, width)
            tile = cpl[:, pl.ds(start, width)]
            tile = pltpu.roll(tile, (yy * span + width - z % NY * span) % width, 1)
            wanted = jnp.where(lane // span == yy, tile, wanted)
        want_v[...] = wanted
        row = lax.broadcasted_iota(jnp.int32, (width, width), 0)
        col = lax.broadcasted_iota(jnp.int32, (width, width), 1)
        slot = pair_index(y, (z + NZ - row // group) % NZ, c) * group + row % group
        held = jnp.zeros((width, width), jnp.int32)
        for r in range(slots.shape[0]):
            held += jnp.where(slots[r : r + 1, :] == slot, col + r * width, 0)
        shift = width // 2
        while shift:
            held += pltpu.roll(held, shift, 1)
            shift //= 2
        place = (row % group // per + NX - x) % NX * per + row % per
        hits = jnp.zeros((width, width), jnp.int32)
        for e in range(nb):
            hits = jnp.maximum(hits, jnp.where(wanted[e : e + 1, :] == held, place, 0))
        best = hits
        for r in range(1, per):
            best = jnp.maximum(best, pltpu.roll(hits, width - r, 1))
        sel_v[...] = jnp.max(best.reshape(NZ, group, width), axis=1)
        a = pltpu.make_async_copy(sel_v, sel, local_sem.at[len(local)])
        b = pltpu.make_async_copy(want_v, want, local_sem.at[len(local) + 1])
        a.start()
        b.start()
        a.wait()
        b.wait()

    def make_entries():
        mine = ((y * NC + c) * NX + x) * per

        def one(i, carry):
            t = slot_of[want[i % nb, mine + i // nb]] // group
            ty, tz, tc = t // (NZ * NC), t // NC % NZ, t % NC
            k = (z - tz + NZ) % NZ
            order = jnp.where(k <= NZ // 2, jnp.maximum(2 * k - 1, 0), 2 * (NZ - k))
            entry[i] = ((y - ty + NY) % NY * NC + (c + tc) % NC) * NZ + order
            return carry

        lax.fori_loop(0, per * nb, one, 0)

    own_rows = pl.ds(pl.multiple_of(x * quarter, quarter), quarter)

    def spread(it, s, count=1):
        slots_in = pl.ds(s, count)
        for d in (1, 3, 2):
            theirs = pl.ds(pl.multiple_of(xs[d] * quarter, quarter), quarter)
            send(
                blocks[it].at[slots_in, theirs],
                gath[it][0].at[pl.ds((NX - d) * per + s, count)],
                x_send.at[it],
                z_recv.at[it, NX - d],
                dev(dx=d),
            )
        gath[it][0][slots_in] = blocks[it][slots_in, own_rows, :]

    def singles_terms(it):
        if it == 0:
            local[3].wait()
            local[7].wait()
        orbital = lax.broadcasted_iota(jnp.int32, (NOCC, width), 0)
        total = jnp.zeros((NOCC, width), jnp.float32)
        for s in range(per):
            row = lax.dot_general(
                jnp.broadcast_to(proj[s : s + 1, :], (8, width)),
                state[s],
                (((1,), (1,)), ((), ())),
                precision=HIGHEST,
                preferred_element_type=jnp.float32,
            )[0:1]
            row = jnp.broadcast_to(row, (NOCC, width))
            total += jnp.where(orbital == orbs[0, s], row, 0.0)
            total += jnp.where(orbital == orbs[1, s], row, 0.0)
        parts[it] = total

    for it in range(ITERS):
        g = gath[it]

        def piece(k, q, g=g):
            return g[k].at[pl.ds(q * per, per)]

        def push(k, q, k2, to, piece=piece, it=it):
            sent.append(send(piece(k, q), piece(k2, q), z_send.at[it], z_recv.at[it, k2 * NX + q], to))

        def ready(k, q, piece=piece, it=it):
            arrived(piece(k, q), z_recv.at[it, k * NX + q])

        def ring(k, k2, to, it=it):
            sent.append(
                send(part_z.at[it, k], part_z.at[it, k2], p_send.at[it, 3], p_recv.at[it, 3 + k2], to)
            )

        def ringed(k, it=it):
            arrived(part_z.at[it, k], p_recv.at[it, 3 + k])

        def deliver(ks, it=it, g=g):
            first, count = FIRST[ks[0]], len(ks)

            for i, (dx, dy, dc) in enumerate(steps):
                at = ((ys[dy] * NC + cs[dc]) * NX + xs[dx]) * per
                for j, k in enumerate(ks):
                    out_buf[it][i, first + j] = g[k][sel[k, at]]
            for j in range(count):
                recv[it][first + j, own_rows, :] = out_buf[it][0, first + j]
            for dx, dy, dc in far_first:
                i = steps.index((dx, dy, dc))
                if i:
                    send(
                        out_buf[it].at[i, pl.ds(first, count)],
                        recv[it].at[pl.ds((dy * NC + dc) * NZ + first, count), own_rows],
                        y_send.at[it],
                        y_recv.at[it],
                        dev(dx, dy, 0, dc),
                    )

        if it == 0:
            singles_terms(0)
            make_tables()
            pl.semaphore_wait(barrier, len(peers))
            spread(0, 0, per)
        push(0, 0, 1, up)
        push(0, 0, 7, down)
        if it:
            singles_terms(it)
        share = NOCC // NC
        mine = pl.ds(pl.multiple_of(c * share, share), share)
        other = pl.ds(pl.multiple_of((1 - c) * share, share), share)
        sent.append(send(parts.at[it, other], half.at[it], p_send.at[it, 0], p_recv.at[it, 0], dev(dc=1)))

        for q in (1, 3, 2):
            ready(0, q)
            push(0, q, 1, up)
            push(0, q, 7, down)
        arrived(half.at[it], p_recv.at[it, 0])
        sums[it, 0] = parts[it, mine, :] + half[it]
        for d in range(1, NY):
            sent.append(send(sums.at[it, 0], part_y.at[it, d - 1], p_send.at[it, 1], p_recv.at[it, 1], dev(dy=d)))
        deliver((0,))

        for q in (0, 1, 3, 2):
            ready(1, q)
            push(1, q, 2, up)
            ready(7, q)
            push(7, q, 6, down)
        arrived(part_y.at[it], p_recv.at[it, 1])
        sums[it, 1] = sums[it, 0] + part_y[it, 0] + part_y[it, 1] + part_y[it, 2]
        for d in range(1, NX):
            sent.append(send(sums.at[it, 1], part_x.at[it, d - 1], p_send.at[it, 2], p_recv.at[it, 2], dev(dx=d)))
        deliver((1, 7))

        for q in (0, 1, 3, 2):
            ready(2, q)
            push(2, q, 3, up)
            ready(6, q)
            push(6, q, 5, down)
        arrived(part_x.at[it], p_recv.at[it, 2])
        part_z[it, 0] = sums[it, 1] + part_x[it, 0] + part_x[it, 1] + part_x[it, 2]
        ring(0, 1, up)
        ring(0, 7, down)
        deliver((2, 6))

        for q in (0, 1, 3, 2):
            ready(3, q)
            if q in (0, 1):
                push(3, q, 4, up)
            ready(5, q)
            if q in (2, 3):
                push(5, q, 4, down)
        ringed(1)
        ring(1, 2, up)
        ringed(7)
        ring(7, 6, down)
        for q in (0, 1, 3, 2):
            ready(4, q)
        deliver((3, 5, 4))

        ringed(2)
        ring(2, 3, up)
        ringed(6)
        ring(6, 5, down)
        if it == 0:
            local[8].wait()
            local[9].wait()
            make_entries()
            local[4].wait()
            for s in range(per):
                e_row = ener[s : s + 1, :]
                den[s] = column(e_row) + e_row
                rden[s] = 1.0 / den[s]
                pcol[s] = column(proj[s : s + 1, :])
            local[5].wait()
        ringed(3)
        ring(3, 4, up)
        ringed(5)
        ringed(4)
        total = part_z[it, 0]
        for k in range(1, NZ):
            total += part_z[it, k]
        full[it, mine, :] = total
        sums[it, 2] = total
        sent.append(send(sums.at[it, 2], half.at[ITERS + it], p_send.at[it, 4], p_recv.at[it, 2 * NX + 3], dev(dc=1)))
        arrived(half.at[ITERS + it], p_recv.at[it, 2 * NX + 3])
        full[it, other, :] = half[ITERS + it]
        if it == ITERS - 1:
            last_copy = pltpu.make_async_copy(state, last_hbm, local_sem.at[len(local) + 3])
            last_copy.start()
        for s in range(per):
            left_row = full[it, pl.ds(orbs[0, s], 1), :]
            right_row = full[it, pl.ds(orbs[1, s], 1), :]
            base[s] = column(left_row) * proj[s : s + 1, :] + pcol[s] * right_row
            if it < ITERS - 1:
                whole = integ[s].astype(jnp.float32) + den[s] * state[s] + base[s]
                base[s] = state[s] - whole / den[s]
        if it == 0:
            local[6].wait()
        arrived(recv[it].at[pl.ds(0, (PLANE - 1) * NZ // NX)], y_recv.at[it])

        def one_slot(s, it=it):
            acc = jnp.zeros((width, width), jnp.float32)
            scaled = [
                (
                    coup[s, k]
                    * jnp.dot(inter[s * nb + k], recv[it][entry[s * nb + k]], preferred_element_type=jnp.float32)
                ).astype(jnp.bfloat16)
                for k in range(nb)
            ]
            for k in range(0, nb, 2):
                acc += lax.dot_general(
                    jnp.concatenate(scaled[k : k + 2], axis=1),
                    jnp.concatenate([inter[s * nb + k], inter[s * nb + k + 1]], axis=1),
                    (((1,), (1,)), ((), ())),
                    preferred_element_type=jnp.float32,
                )
            if it == ITERS - 1:
                change[s] = base[s] - acc
                pltpu.make_async_copy(change.at[s], change_hbm.at[s], local_sem.at[len(local) + 2]).start()
            else:
                new = base[s] + acc * rden[s]
                state[s] = new
                blocks[it + 1][s] = new.astype(jnp.bfloat16)
                spread(it + 1, s)

        for s in range(per):
            one_slot(s)

    last_copy.wait()
    pltpu.make_async_copy(change, change_hbm, local_sem.at[len(local) + 2]).wait()
    for copy in sent:
        copy.wait_send()
    for it in range(ITERS):
        arrived(gath[it][0].at[pl.ds(0, group - per)], x_send.at[it])
        sends = recv[it].at[pl.ds(0, (PLANE - 1) * NZ // NX)]
        arrived(sends, y_send.at[it])


def body(amplitudes, integrals, energies, intersections, couplings, projector, pair_orbitals, coupled, pair_slot):
    per, width, _ = amplitudes.shape
    nb = coupled.shape[1]
    total = pair_slot.shape[0]
    group = NX * per
    quarter = width // NX
    bf16, f32, i32 = jnp.bfloat16, jnp.float32, jnp.int32
    smem = pl.BlockSpec(memory_space=pltpu.SMEM)
    hbm = pl.BlockSpec(memory_space=pltpu.HBM)
    dma = pltpu.SemaphoreType.DMA
    square = (per, width, width)
    share = NOCC // NC
    scratch = [pltpu.VMEM((group, quarter, width), bf16) for _ in range(2 * NZ)]
    scratch += [pltpu.VMEM((PLANE, NZ, quarter, width), bf16) for _ in range(2)]
    scratch += [pltpu.VMEM((NZ * NY * NC, width, width), bf16) for _ in range(2)]
    scratch += [pltpu.VMEM(square, bf16) for _ in range(2)]
    scratch += [
        pltpu.VMEM((ITERS, NOCC, width), f32),
        pltpu.VMEM((ITERS, NOCC, width), f32),
        pltpu.VMEM((2 * ITERS, share, width), f32),
        pltpu.VMEM((ITERS, NY - 1, share, width), f32),
        pltpu.VMEM((ITERS, NX - 1, share, width), f32),
        pltpu.VMEM((ITERS, NZ, share, width), f32),
        pltpu.VMEM((ITERS, 4, share, width), f32),
        pltpu.VMEM((per * nb, width, width), bf16),
        pltpu.VMEM(square, bf16),
        pltpu.VMEM(square, f32),
        pltpu.VMEM((per, width), f32),
        pltpu.VMEM((per, width), f32),
        pltpu.VMEM((nb, total), i32),
        pltpu.VMEM((total // width, width), i32),
        pltpu.VMEM(square, f32),
        pltpu.VMEM(square, f32),
        pltpu.VMEM(square, f32),
        pltpu.VMEM(square, f32),
        pltpu.VMEM(square, f32),
        pltpu.VMEM((NZ, width), i32),
        pltpu.VMEM((nb, width), i32),
        pltpu.SMEM((NZ, width), i32),
        pltpu.SMEM((nb, width), i32),
        pltpu.SMEM((per * nb,), i32),
        pltpu.SMEM((per, nb), f32),
        pltpu.SMEM((2, per), i32),
        pltpu.SMEM((total,), i32),
        dma((14,)),
        dma((ITERS,)),
        dma((ITERS,)),
        dma((ITERS, NX * NZ)),
        dma((ITERS,)),
        dma((ITERS,)),
        dma((ITERS, 5)),
        dma((ITERS, NZ + 4)),
    ]
    last, change = pl.pallas_call(
        kernel,
        out_shape=(
            jax.ShapeDtypeStruct(square, f32),
            jax.ShapeDtypeStruct(square, f32),
        ),
        in_specs=[hbm, hbm, hbm, hbm, hbm, hbm, hbm, hbm, hbm, hbm],
        out_specs=(hbm, hbm),
        scratch_shapes=scratch,
        compiler_params=pltpu.CompilerParams(
            collective_id=0, has_side_effects=True, vmem_limit_bytes=67043328
        ),
    )(
        couplings,
        pair_orbitals.T,
        pair_slot,
        amplitudes,
        integrals,
        energies,
        intersections.reshape(per * nb, width, width),
        projector,
        coupled.T,
        pair_slot.reshape(total // width, width),
    )
    denom = energies[:, :, None] + energies[:, None, :]
    residual = integrals.astype(f32) + denom * last + change
    return (last - residual / denom, residual)


def solution(mesh):
    both = ("pairs", "orb")
    return jax.shard_map(
        body,
        mesh=mesh,
        in_specs=(
            P(both, None, None),
            P(both, None, None),
            P(both, None),
            P(both, None, None, None),
            P(both, None),
            P(both, None),
            P(both, None),
            P(),
            P(),
        ),
        out_specs=(P(both, None, None), P(both, None, None)),
        check_vma=False,
    )
```

```python
import jax
import jax.numpy as jnp
from jax import lax
from jax.experimental import pallas as pl
from jax.experimental.pallas import tpu as pltpu
from jax.sharding import PartitionSpec as P

ITERS = 2
NOCC = 32
NX, NY, NZ, NC = 4, 4, 8, 2
PLANE = NX * NY * NC
MESH = pl.DeviceIdType.MESH
HIGHEST = lax.Precision.HIGHEST
ROUNDS = ((0,), (1, 7), (2, 6), (3, 5, 4))
FIRST = {0: 0, 1: 1, 2: 3, 3: 5}


def pair_index(y, z, c):
    return (y * NZ + z) * NC + c


def kernel(
    coup_hbm, orbs_hbm, slot_hbm, amp_hbm, integ_hbm, ener_hbm, inter_hbm, proj_hbm, coupled_hbm, slots_hbm, last_hbm, change_hbm,
    *scratch,
):
    gath = [scratch[0:NZ], scratch[NZ : 2 * NZ]]
    out_buf = scratch[2 * NZ : 2 * NZ + 2]
    recv = scratch[2 * NZ + 2 : 2 * NZ + 4]
    blocks = scratch[2 * NZ + 4 : 2 * NZ + 6]
    (parts, full, half, part_y, part_x, part_z, sums, inter, integ, state, ener, proj, cpl, slots, den, rden, pcol, base, change,
     sel_v, want_v, sel, want, entry, coup, orbs, slot_of,
     local_sem, x_send, z_send, z_recv, y_send, y_recv, p_send, p_recv) = scratch[2 * NZ + 6 :]
    per, width, _ = state.shape
    nb = inter.shape[0] // per
    group = NX * per
    quarter = width // NX
    pair_idx = lax.axis_index("pairs")
    x = lax.axis_index("orb")
    y, z, c = pair_idx // (NZ * NC), pair_idx // NC % NZ, pair_idx % NC

    xs = [(x + d) % NX for d in range(NX)]
    ys = [(y + d) % NY for d in range(NY)]
    zs = [(z + d) % NZ for d in range(NZ)]
    cs = [(c + d) % NC for d in range(NC)]

    def dev(dx=0, dy=0, dz=0, dc=0):
        return (pair_index(ys[dy], zs[dz], cs[dc]), xs[dx])

    steps = [(dx, dy, dc) for dx in range(NX) for dy in range(NY) for dc in range(NC)]
    far_first = sorted(steps, key=lambda t: -(min(t[0], NX - t[0]) + min(t[1], NY - t[1])))

    local = [
        pltpu.make_async_copy(a, b, local_sem.at[i])
        for i, (a, b) in enumerate(
            (
                (amp_hbm, state),
                (coupled_hbm, cpl),
                (slots_hbm, slots),
                (proj_hbm, proj),
                (ener_hbm, ener),
                (integ_hbm, integ),
                (inter_hbm, inter),
                (orbs_hbm, orbs),
                (slot_hbm, slot_of),
                (coup_hbm, coup),
            )
        )
    ]
    for copy in local:
        copy.start()

    barrier = pltpu.get_barrier_semaphore()

    up, down = dev(dz=1), dev(dz=NZ - 1)
    peers = [up, down]
    peers += [dev(dx, dy, 0, dc) for dx, dy, dc in far_first if (dx, dy, dc) != (0, 0, 0)]
    for peer in peers:
        pl.semaphore_signal(barrier, inc=1, device_id=peer, device_id_type=MESH)

    local[0].wait()
    for s in range(per):
        blocks[0][s] = state[s].astype(jnp.bfloat16)

    sent = []

    def send(src, dst, ssem, rsem, to):
        copy = pltpu.make_async_remote_copy(
            src_ref=src, dst_ref=dst, send_sem=ssem, recv_sem=rsem, device_id=to, device_id_type=MESH
        )
        copy.start()
        return copy

    def arrived(ref, sem):
        pltpu.make_async_copy(ref, ref, sem).wait()

    def column(row):
        return jnp.broadcast_to(row, (width, width)).T

    def make_tables():
        local[1].wait()
        local[2].wait()
        lane = lax.broadcasted_iota(jnp.int32, (nb, width), 1)
        span = width // NY
        wanted = jnp.zeros((nb, width), jnp.int32)
        for yy in range(NY):
            start = pl.multiple_of(yy * (NZ * span) + z // NY * width, width)
            tile = cpl[:, pl.ds(start, width)]
            tile = pltpu.roll(tile, (yy * span + width - z % NY * span) % width, 1)
            wanted = jnp.where(lane // span == yy, tile, wanted)
        want_v[...] = wanted
        row = lax.broadcasted_iota(jnp.int32, (width, width), 0)
        col = lax.broadcasted_iota(jnp.int32, (width, width), 1)
        slot = pair_index(y, (z + NZ - row // group) % NZ, c) * group + row % group
        held = jnp.zeros((width, width), jnp.int32)
        for r in range(slots.shape[0]):
            held += jnp.where(slots[r : r + 1, :] == slot, col + r * width, 0)
        shift = width // 2
        while shift:
            held += pltpu.roll(held, shift, 1)
            shift //= 2
        place = (row % group // per + NX - x) % NX * per + row % per
        hits = jnp.zeros((width, width), jnp.int32)
        for e in range(nb):
            hits = jnp.maximum(hits, jnp.where(wanted[e : e + 1, :] == held, place, 0))
        best = hits
        for r in range(1, per):
            best = jnp.maximum(best, pltpu.roll(hits, width - r, 1))
        sel_v[...] = jnp.max(best.reshape(NZ, group, width), axis=1)
        a = pltpu.make_async_copy(sel_v, sel, local_sem.at[len(local)])
        b = pltpu.make_async_copy(want_v, want, local_sem.at[len(local) + 1])
        a.start()
        b.start()
        a.wait()
        b.wait()

    def make_entries():
        mine = ((y * NC + c) * NX + x) * per

        def one(i, carry):
            t = slot_of[want[i % nb, mine + i // nb]] // group
            ty, tz, tc = t // (NZ * NC), t // NC % NZ, t % NC
            k = (z - tz + NZ) % NZ
            order = jnp.where(k <= NZ // 2, jnp.maximum(2 * k - 1, 0), 2 * (NZ - k))
            entry[i] = ((y - ty + NY) % NY * NC + (c + tc) % NC) * NZ + order
            return carry

        lax.fori_loop(0, per * nb, one, 0)

    own_rows = pl.ds(pl.multiple_of(x * quarter, quarter), quarter)

    def spread(it, s, count=1):
        slots_in = pl.ds(s, count)
        for d in (1, 3, 2):
            theirs = pl.ds(pl.multiple_of(xs[d] * quarter, quarter), quarter)
            send(
                blocks[it].at[slots_in, theirs],
                gath[it][0].at[pl.ds((NX - d) * per + s, count)],
                x_send.at[it],
                z_recv.at[it, NX - d],
                dev(dx=d),
            )
        gath[it][0][slots_in] = blocks[it][slots_in, own_rows, :]

    def singles_terms(it):
        if it == 0:
            local[3].wait()
            local[7].wait()
        orbital = lax.broadcasted_iota(jnp.int32, (NOCC, width), 0)
        total = jnp.zeros((NOCC, width), jnp.float32)
        for s in range(per):
            row = lax.dot_general(
                jnp.broadcast_to(proj[s : s + 1, :], (8, width)),
                state[s],
                (((1,), (1,)), ((), ())),
                precision=HIGHEST,
                preferred_element_type=jnp.float32,
            )[0:1]
            row = jnp.broadcast_to(row, (NOCC, width))
            total += jnp.where(orbital == orbs[0, s], row, 0.0)
            total += jnp.where(orbital == orbs[1, s], row, 0.0)
        parts[it] = total

    for it in range(ITERS):
        g = gath[it]

        def piece(k, q, g=g):
            return g[k].at[pl.ds(q * per, per)]

        def push(k, q, k2, to, piece=piece, it=it):
            sent.append(send(piece(k, q), piece(k2, q), z_send.at[it], z_recv.at[it, k2 * NX + q], to))

        def ready(k, q, piece=piece, it=it):
            arrived(piece(k, q), z_recv.at[it, k * NX + q])

        def ring(k, k2, to, it=it):
            sent.append(
                send(part_z.at[it, k], part_z.at[it, k2], p_send.at[it, 3], p_recv.at[it, 3 + k2], to)
            )

        def ringed(k, it=it):
            arrived(part_z.at[it, k], p_recv.at[it, 3 + k])

        def deliver(ks, it=it, g=g):
            first, count = FIRST[ks[0]], len(ks)

            for i, (dx, dy, dc) in enumerate(steps):
                at = ((ys[dy] * NC + cs[dc]) * NX + xs[dx]) * per
                for j, k in enumerate(ks):
                    out_buf[it][i, first + j] = g[k][sel[k, at]]
            for j in range(count):
                recv[it][first + j, own_rows, :] = out_buf[it][0, first + j]
            for dx, dy, dc in far_first:
                i = steps.index((dx, dy, dc))
                if i:
                    send(
                        out_buf[it].at[i, pl.ds(first, count)],
                        recv[it].at[pl.ds((dy * NC + dc) * NZ + first, count), own_rows],
                        y_send.at[it],
                        y_recv.at[it],
                        dev(dx, dy, 0, dc),
                    )

        if it == 0:
            singles_terms(0)
            pl.semaphore_wait(barrier, len(peers))
            spread(0, 0, per)
        push(0, 0, 1, up)
        push(0, 0, 7, down)
        if it:
            singles_terms(it)
        share = NOCC // NC
        mine = pl.ds(pl.multiple_of(c * share, share), share)
        other = pl.ds(pl.multiple_of((1 - c) * share, share), share)
        sent.append(send(parts.at[it, other], half.at[it], p_send.at[it, 0], p_recv.at[it, 0], dev(dc=1)))
        if it == 0:
            make_tables()

        for q in (1, 3, 2):
            ready(0, q)
            push(0, q, 1, up)
            push(0, q, 7, down)
        arrived(half.at[it], p_recv.at[it, 0])
        sums[it, 0] = parts[it, mine, :] + half[it]
        for d in range(1, NY):
            sent.append(send(sums.at[it, 0], part_y.at[it, d - 1], p_send.at[it, 1], p_recv.at[it, 1], dev(dy=d)))
        deliver((0,))

        for q in (0, 1, 3, 2):
            ready(1, q)
            push(1, q, 2, up)
            ready(7, q)
            push(7, q, 6, down)
        arrived(part_y.at[it], p_recv.at[it, 1])
        sums[it, 1] = sums[it, 0] + part_y[it, 0] + part_y[it, 1] + part_y[it, 2]
        for d in range(1, NX):
            sent.append(send(sums.at[it, 1], part_x.at[it, d - 1], p_send.at[it, 2], p_recv.at[it, 2], dev(dx=d)))
        deliver((1, 7))

        for q in (0, 1, 3, 2):
            ready(2, q)
            push(2, q, 3, up)
            ready(6, q)
            push(6, q, 5, down)
        arrived(part_x.at[it], p_recv.at[it, 2])
        part_z[it, 0] = sums[it, 1] + part_x[it, 0] + part_x[it, 1] + part_x[it, 2]
        ring(0, 1, up)
        ring(0, 7, down)
        deliver((2, 6))

        for q in (0, 1, 3, 2):
            ready(3, q)
            if q in (0, 1):
                push(3, q, 4, up)
            ready(5, q)
            if q in (2, 3):
                push(5, q, 4, down)
        ringed(1)
        ring(1, 2, up)
        ringed(7)
        ring(7, 6, down)
        for q in (0, 1, 3, 2):
            ready(4, q)
        deliver((3, 5, 4))

        ringed(2)
        ring(2, 3, up)
        ringed(6)
        ring(6, 5, down)
        if it == 0:
            local[8].wait()
            local[9].wait()
            make_entries()
            local[4].wait()
            for s in range(per):
                e_row = ener[s : s + 1, :]
                den[s] = column(e_row) + e_row
                rden[s] = 1.0 / den[s]
                pcol[s] = column(proj[s : s + 1, :])
            local[5].wait()
        ringed(3)
        ring(3, 4, up)
        ringed(5)
        ringed(4)
        total = part_z[it, 0]
        for k in range(1, NZ):
            total += part_z[it, k]
        full[it, mine, :] = total
        sums[it, 2] = total
        sent.append(send(sums.at[it, 2], half.at[ITERS + it], p_send.at[it, 4], p_recv.at[it, 2 * NX + 3], dev(dc=1)))
        arrived(half.at[ITERS + it], p_recv.at[it, 2 * NX + 3])
        full[it, other, :] = half[ITERS + it]
        if it == ITERS - 1:
            last_copy = pltpu.make_async_copy(state, last_hbm, local_sem.at[len(local) + 3])
            last_copy.start()
        for s in range(per):
            left_row = full[it, pl.ds(orbs[0, s], 1), :]
            right_row = full[it, pl.ds(orbs[1, s], 1), :]
            base[s] = column(left_row) * proj[s : s + 1, :] + pcol[s] * right_row
            if it < ITERS - 1:
                whole = integ[s].astype(jnp.float32) + den[s] * state[s] + base[s]
                base[s] = state[s] - whole / den[s]
        if it == 0:
            local[6].wait()
        arrived(recv[it].at[pl.ds(0, (PLANE - 1) * NZ // NX)], y_recv.at[it])

        def one_slot(s, it=it):
            acc = jnp.zeros((width, width), jnp.float32)
            scaled = [
                (
                    coup[s, k]
                    * jnp.dot(inter[s * nb + k], recv[it][entry[s * nb + k]], preferred_element_type=jnp.float32)
                ).astype(jnp.bfloat16)
                for k in range(nb)
            ]
            for k in range(0, nb, 2):
                acc += lax.dot_general(
                    jnp.concatenate(scaled[k : k + 2], axis=1),
                    jnp.concatenate([inter[s * nb + k], inter[s * nb + k + 1]], axis=1),
                    (((1,), (1,)), ((), ())),
                    preferred_element_type=jnp.float32,
                )
            if it == ITERS - 1:
                change[s] = base[s] - acc
                pltpu.make_async_copy(change.at[s], change_hbm.at[s], local_sem.at[len(local) + 2]).start()
            else:
                new = base[s] + acc * rden[s]
                state[s] = new
                blocks[it + 1][s] = new.astype(jnp.bfloat16)
                spread(it + 1, s)

        for s in range(per):
            one_slot(s)

    last_copy.wait()
    pltpu.make_async_copy(change, change_hbm, local_sem.at[len(local) + 2]).wait()
    for copy in sent:
        copy.wait_send()
    for it in range(ITERS):
        arrived(gath[it][0].at[pl.ds(0, group - per)], x_send.at[it])
        sends = recv[it].at[pl.ds(0, (PLANE - 1) * NZ // NX)]
        arrived(sends, y_send.at[it])


def body(amplitudes, integrals, energies, intersections, couplings, projector, pair_orbitals, coupled, pair_slot):
    per, width, _ = amplitudes.shape
    nb = coupled.shape[1]
    total = pair_slot.shape[0]
    group = NX * per
    quarter = width // NX
    bf16, f32, i32 = jnp.bfloat16, jnp.float32, jnp.int32
    smem = pl.BlockSpec(memory_space=pltpu.SMEM)
    hbm = pl.BlockSpec(memory_space=pltpu.HBM)
    dma = pltpu.SemaphoreType.DMA
    square = (per, width, width)
    share = NOCC // NC
    scratch = [pltpu.VMEM((group, quarter, width), bf16) for _ in range(2 * NZ)]
    scratch += [pltpu.VMEM((PLANE, NZ, quarter, width), bf16) for _ in range(2)]
    scratch += [pltpu.VMEM((NZ * NY * NC, width, width), bf16) for _ in range(2)]
    scratch += [pltpu.VMEM(square, bf16) for _ in range(2)]
    scratch += [
        pltpu.VMEM((ITERS, NOCC, width), f32),
        pltpu.VMEM((ITERS, NOCC, width), f32),
        pltpu.VMEM((2 * ITERS, share, width), f32),
        pltpu.VMEM((ITERS, NY - 1, share, width), f32),
        pltpu.VMEM((ITERS, NX - 1, share, width), f32),
        pltpu.VMEM((ITERS, NZ, share, width), f32),
        pltpu.VMEM((ITERS, 4, share, width), f32),
        pltpu.VMEM((per * nb, width, width), bf16),
        pltpu.VMEM(square, bf16),
        pltpu.VMEM(square, f32),
        pltpu.VMEM((per, width), f32),
        pltpu.VMEM((per, width), f32),
        pltpu.VMEM((nb, total), i32),
        pltpu.VMEM((total // width, width), i32),
        pltpu.VMEM(square, f32),
        pltpu.VMEM(square, f32),
        pltpu.VMEM(square, f32),
        pltpu.VMEM(square, f32),
        pltpu.VMEM(square, f32),
        pltpu.VMEM((NZ, width), i32),
        pltpu.VMEM((nb, width), i32),
        pltpu.SMEM((NZ, width), i32),
        pltpu.SMEM((nb, width), i32),
        pltpu.SMEM((per * nb,), i32),
        pltpu.SMEM((per, nb), f32),
        pltpu.SMEM((2, per), i32),
        pltpu.SMEM((total,), i32),
        dma((14,)),
        dma((ITERS,)),
        dma((ITERS,)),
        dma((ITERS, NX * NZ)),
        dma((ITERS,)),
        dma((ITERS,)),
        dma((ITERS, 5)),
        dma((ITERS, NZ + 4)),
    ]
    last, change = pl.pallas_call(
        kernel,
        out_shape=(
            jax.ShapeDtypeStruct(square, f32),
            jax.ShapeDtypeStruct(square, f32),
        ),
        in_specs=[hbm, hbm, hbm, hbm, hbm, hbm, hbm, hbm, hbm, hbm],
        out_specs=(hbm, hbm),
        scratch_shapes=scratch,
        compiler_params=pltpu.CompilerParams(
            collective_id=0, has_side_effects=True, vmem_limit_bytes=67043328
        ),
    )(
        couplings,
        pair_orbitals.T,
        pair_slot,
        amplitudes,
        integrals,
        energies,
        intersections.reshape(per * nb, width, width),
        projector,
        coupled.T,
        pair_slot.reshape(total // width, width),
    )
    denom = energies[:, :, None] + energies[:, None, :]
    residual = integrals.astype(f32) + denom * last + change
    return (last - residual / denom, residual)


def solution(mesh):
    both = ("pairs", "orb")
    return jax.shard_map(
        body,
        mesh=mesh,
        in_specs=(
            P(both, None, None),
            P(both, None, None),
            P(both, None),
            P(both, None, None, None),
            P(both, None),
            P(both, None),
            P(both, None),
            P(),
            P(),
        ),
        out_specs=(P(both, None, None), P(both, None, None)),
        check_vma=False,
    )
```

```python
import jax
import jax.numpy as jnp
from jax import lax
from jax.experimental import pallas as pl
from jax.experimental.pallas import tpu as pltpu
from jax.sharding import PartitionSpec as P

ITERS = 2
NOCC = 32
NX, NY, NZ, NC = 4, 4, 8, 2
PLANE = NX * NY * NC
MESH = pl.DeviceIdType.MESH
HIGHEST = lax.Precision.HIGHEST
ROUNDS = ((0,), (1, 7), (2, 6), (3, 5, 4))
FIRST = {0: 0, 1: 1, 2: 3, 3: 5}


def pair_index(y, z, c):
    return (y * NZ + z) * NC + c


def kernel(
    coup_hbm, orbs_hbm, slot_hbm, amp_hbm, integ_hbm, ener_hbm, inter_hbm, proj_hbm, coupled_hbm, slots_hbm, last_hbm, change_hbm,
    *scratch,
):
    gath = [scratch[0:NZ], scratch[NZ : 2 * NZ]]
    out_buf = scratch[2 * NZ : 2 * NZ + 2]
    recv = scratch[2 * NZ + 2 : 2 * NZ + 4]
    blocks = scratch[2 * NZ + 4 : 2 * NZ + 6]
    (parts, full, half, part_y, part_x, part_z, sums, inter, integ, state, ener, proj, cpl, slots, den, rden, pcol, base, change,
     sel_v, want_v, sel, want, entry, coup, orbs, slot_of,
     local_sem, x_send, z_send, z_recv, y_send, y_recv, p_send, p_recv) = scratch[2 * NZ + 6 :]
    per, width, _ = state.shape
    nb = inter.shape[0] // per
    group = NX * per
    quarter = width // NX
    pair_idx = lax.axis_index("pairs")
    x = lax.axis_index("orb")
    y, z, c = pair_idx // (NZ * NC), pair_idx // NC % NZ, pair_idx % NC

    xs = [(x + d) % NX for d in range(NX)]
    ys = [(y + d) % NY for d in range(NY)]
    zs = [(z + d) % NZ for d in range(NZ)]
    cs = [(c + d) % NC for d in range(NC)]

    def dev(dx=0, dy=0, dz=0, dc=0):
        return (pair_index(ys[dy], zs[dz], cs[dc]), xs[dx])

    steps = [(dx, dy, dc) for dx in range(NX) for dy in range(NY) for dc in range(NC)]
    far_first = sorted(steps, key=lambda t: -(min(t[0], NX - t[0]) + min(t[1], NY - t[1])))

    local = [
        pltpu.make_async_copy(a, b, local_sem.at[i])
        for i, (a, b) in enumerate(
            (
                (amp_hbm, state),
                (coupled_hbm, cpl),
                (slots_hbm, slots),
                (proj_hbm, proj),
                (ener_hbm, ener),
                (integ_hbm, integ),
                (inter_hbm, inter),
                (orbs_hbm, orbs),
                (slot_hbm, slot_of),
                (coup_hbm, coup),
            )
        )
    ]
    for copy in local:
        copy.start()

    barrier = pltpu.get_barrier_semaphore()

    up, down = dev(dz=1), dev(dz=NZ - 1)
    peers = [up, down]
    peers += [dev(dx, dy, 0, dc) for dx, dy, dc in far_first if (dx, dy, dc) != (0, 0, 0)]
    for peer in peers:
        pl.semaphore_signal(barrier, inc=1, device_id=peer, device_id_type=MESH)

    local[0].wait()
    for s in range(per):
        blocks[0][s] = state[s].astype(jnp.bfloat16)

    sent = []

    def send(src, dst, ssem, rsem, to):
        copy = pltpu.make_async_remote_copy(
            src_ref=src, dst_ref=dst, send_sem=ssem, recv_sem=rsem, device_id=to, device_id_type=MESH
        )
        copy.start()
        return copy

    def arrived(ref, sem):
        pltpu.make_async_copy(ref, ref, sem).wait()

    def column(row):
        return jnp.broadcast_to(row, (width, width)).T

    def make_tables():
        local[1].wait()
        local[2].wait()
        lane = lax.broadcasted_iota(jnp.int32, (nb, width), 1)
        span = width // NY
        wanted = jnp.zeros((nb, width), jnp.int32)
        for yy in range(NY):
            start = pl.multiple_of(yy * (NZ * span) + z // NY * width, width)
            tile = cpl[:, pl.ds(start, width)]
            tile = pltpu.roll(tile, (yy * span + width - z % NY * span) % width, 1)
            wanted = jnp.where(lane // span == yy, tile, wanted)
        want_v[...] = wanted
        row = lax.broadcasted_iota(jnp.int32, (width, width), 0)
        col = lax.broadcasted_iota(jnp.int32, (width, width), 1)
        slot = pair_index(y, (z + NZ - row // group) % NZ, c) * group + row % group
        held = jnp.zeros((width, width), jnp.int32)
        for r in range(slots.shape[0]):
            held += jnp.where(slots[r : r + 1, :] == slot, col + r * width, 0)
        shift = width // 2
        while shift:
            held += pltpu.roll(held, shift, 1)
            shift //= 2
        place = (row % group // per + NX - x) % NX * per + row % per
        hits = jnp.zeros((width, width), jnp.int32)
        for e in range(nb):
            hits = jnp.maximum(hits, jnp.where(wanted[e : e + 1, :] == held, place, 0))
        best = hits
        for r in range(1, per):
            best = jnp.maximum(best, pltpu.roll(hits, width - r, 1))
        sel_v[...] = jnp.max(best.reshape(NZ, group, width), axis=1)
        a = pltpu.make_async_copy(sel_v, sel, local_sem.at[len(local)])
        b = pltpu.make_async_copy(want_v, want, local_sem.at[len(local) + 1])
        a.start()
        b.start()
        a.wait()
        b.wait()

    def make_entries():
        mine = ((y * NC + c) * NX + x) * per

        def one(i, carry):
            t = slot_of[want[i % nb, mine + i // nb]] // group
            ty, tz, tc = t // (NZ * NC), t // NC % NZ, t % NC
            k = (z - tz + NZ) % NZ
            order = jnp.where(k <= NZ // 2, jnp.maximum(2 * k - 1, 0), 2 * (NZ - k))
            entry[i] = ((y - ty + NY) % NY * NC + (c + tc) % NC) * NZ + order
            return carry

        lax.fori_loop(0, per * nb, one, 0)

    own_rows = pl.ds(pl.multiple_of(x * quarter, quarter), quarter)

    def spread(it, s, count=1):
        slots_in = pl.ds(s, count)
        for d in (1, 3, 2):
            theirs = pl.ds(pl.multiple_of(xs[d] * quarter, quarter), quarter)
            send(
                blocks[it].at[slots_in, theirs],
                gath[it][0].at[pl.ds((NX - d) * per + s, count)],
                x_send.at[it],
                z_recv.at[it, NX - d],
                dev(dx=d),
            )
        gath[it][0][slots_in] = blocks[it][slots_in, own_rows, :]

    def singles_terms(it):
        if it == 0:
            local[3].wait()
            local[7].wait()
        orbital = lax.broadcasted_iota(jnp.int32, (NOCC, width), 0)
        total = jnp.zeros((NOCC, width), jnp.float32)
        for s in range(per):
            row = lax.dot_general(
                jnp.broadcast_to(proj[s : s + 1, :], (8, width)),
                state[s],
                (((1,), (1,)), ((), ())),
                precision=HIGHEST,
                preferred_element_type=jnp.float32,
            )[0:1]
            row = jnp.broadcast_to(row, (NOCC, width))
            total += jnp.where(orbital == orbs[0, s], row, 0.0)
            total += jnp.where(orbital == orbs[1, s], row, 0.0)
        parts[it] = total

    for it in range(ITERS):
        g = gath[it]

        def piece(k, q, g=g):
            return g[k].at[pl.ds(q * per, per)]

        def push(k, q, k2, to, piece=piece, it=it):
            sent.append(send(piece(k, q), piece(k2, q), z_send.at[it], z_recv.at[it, k2 * NX + q], to))

        def ready(k, q, piece=piece, it=it):
            arrived(piece(k, q), z_recv.at[it, k * NX + q])

        def ring(k, k2, to, it=it):
            sent.append(
                send(part_z.at[it, k], part_z.at[it, k2], p_send.at[it, 3], p_recv.at[it, 3 + k2], to)
            )

        def ringed(k, it=it):
            arrived(part_z.at[it, k], p_recv.at[it, 3 + k])

        def deliver(ks, it=it, g=g):
            first, count = FIRST[ks[0]], len(ks)

            for i, (dx, dy, dc) in enumerate(steps):
                at = ((ys[dy] * NC + cs[dc]) * NX + xs[dx]) * per
                for j, k in enumerate(ks):
                    out_buf[it][i, first + j] = g[k][sel[k, at]]
            for j in range(count):
                recv[it][first + j, own_rows, :] = out_buf[it][0, first + j]
            for dx, dy, dc in far_first:
                i = steps.index((dx, dy, dc))
                if i:
                    send(
                        out_buf[it].at[i, pl.ds(first, count)],
                        recv[it].at[pl.ds((dy * NC + dc) * NZ + first, count), own_rows],
                        y_send.at[it],
                        y_recv.at[it],
                        dev(dx, dy, 0, dc),
                    )

        if it == 0:
            singles_terms(0)
            pl.semaphore_wait(barrier, len(peers))
            spread(0, 0, per)
        push(0, 0, 1, up)
        push(0, 0, 7, down)
        if it:
            singles_terms(it)
        share = NOCC // NC
        mine = pl.ds(pl.multiple_of(c * share, share), share)
        other = pl.ds(pl.multiple_of((1 - c) * share, share), share)
        sent.append(send(parts.at[it, other], half.at[it], p_send.at[it, 0], p_recv.at[it, 0], dev(dc=1)))
        if it == 0:
            make_tables()

        for q in (1, 3, 2):
            ready(0, q)
            push(0, q, 1, up)
            push(0, q, 7, down)
        arrived(half.at[it], p_recv.at[it, 0])
        sums[it, 0] = parts[it, mine, :] + half[it]
        for d in range(1, NY):
            sent.append(send(sums.at[it, 0], part_y.at[it, d - 1], p_send.at[it, 1], p_recv.at[it, 1], dev(dy=d)))
        deliver((0,))

        for q in (0, 1, 3, 2):
            ready(1, q)
            push(1, q, 2, up)
            ready(7, q)
            push(7, q, 6, down)
        arrived(part_y.at[it], p_recv.at[it, 1])
        sums[it, 1] = sums[it, 0] + part_y[it, 0] + part_y[it, 1] + part_y[it, 2]
        for d in range(1, NX):
            sent.append(send(sums.at[it, 1], part_x.at[it, d - 1], p_send.at[it, 2], p_recv.at[it, 2], dev(dx=d)))
        deliver((1, 7))

        for q in (0, 1, 3, 2):
            ready(2, q)
            push(2, q, 3, up)
            ready(6, q)
            push(6, q, 5, down)
        arrived(part_x.at[it], p_recv.at[it, 2])
        part_z[it, 0] = sums[it, 1] + part_x[it, 0] + part_x[it, 1] + part_x[it, 2]
        ring(0, 1, up)
        ring(0, 7, down)
        deliver((2, 6))

        for q in (0, 1, 3, 2):
            ready(3, q)
            if q in (0, 1):
                push(3, q, 4, up)
            ready(5, q)
            if q in (2, 3):
                push(5, q, 4, down)
        ringed(1)
        ring(1, 2, up)
        ringed(7)
        ring(7, 6, down)
        for q in (0, 1, 3, 2):
            ready(4, q)
        deliver((3, 5, 4))

        ringed(2)
        ring(2, 3, up)
        ringed(6)
        ring(6, 5, down)
        if it == 0:
            local[8].wait()
            local[9].wait()
            make_entries()
            local[4].wait()
            for s in range(per):
                e_row = ener[s : s + 1, :]
                den[s] = column(e_row) + e_row
                rden[s] = 1.0 / den[s]
                pcol[s] = column(proj[s : s + 1, :])
            local[5].wait()
        ringed(3)
        ring(3, 4, up)
        ringed(5)
        ringed(4)
        total = part_z[it, 0]
        for k in range(1, NZ):
            total += part_z[it, k]
        full[it, mine, :] = total
        sums[it, 2] = total
        sent.append(send(sums.at[it, 2], half.at[ITERS + it], p_send.at[it, 4], p_recv.at[it, 2 * NX + 3], dev(dc=1)))
        arrived(half.at[ITERS + it], p_recv.at[it, 2 * NX + 3])
        full[it, other, :] = half[ITERS + it]
        if it == ITERS - 1:
            last_copy = pltpu.make_async_copy(state, last_hbm, local_sem.at[len(local) + 3])
            last_copy.start()
        for s in range(per):
            left_row = full[it, pl.ds(orbs[0, s], 1), :]
            right_row = full[it, pl.ds(orbs[1, s], 1), :]
            base[s] = column(left_row) * proj[s : s + 1, :] + pcol[s] * right_row
            if it < ITERS - 1:
                whole = integ[s].astype(jnp.float32) + den[s] * state[s] + base[s]
                base[s] = state[s] - whole / den[s]
        if it == 0:
            local[6].wait()
        arrived(recv[it].at[pl.ds(0, (PLANE - 1) * NZ // NX)], y_recv.at[it])

        def one_slot(s, it=it):
            acc = jnp.zeros((width, width), jnp.float32)
            zero = jnp.zeros((width, width), jnp.bfloat16)
            scaled = []
            for k in range(0, nb, 2):
                own = jnp.concatenate([inter[s * nb + k], inter[s * nb + k + 1]], axis=1)
                one = jnp.concatenate([recv[it][entry[s * nb + k]], zero], axis=1)
                two = jnp.concatenate([zero, recv[it][entry[s * nb + k + 1]]], axis=1)
                lifted = jnp.dot(own, jnp.concatenate([one, two], axis=0), preferred_element_type=jnp.float32)
                scaled += [
                    (coup[s, k] * lifted[:, :width]).astype(jnp.bfloat16),
                    (coup[s, k + 1] * lifted[:, width:]).astype(jnp.bfloat16),
                ]
            for k in range(0, nb, 2):
                acc += lax.dot_general(
                    jnp.concatenate(scaled[k : k + 2], axis=1),
                    jnp.concatenate([inter[s * nb + k], inter[s * nb + k + 1]], axis=1),
                    (((1,), (1,)), ((), ())),
                    preferred_element_type=jnp.float32,
                )
            if it == ITERS - 1:
                change[s] = base[s] - acc
                pltpu.make_async_copy(change.at[s], change_hbm.at[s], local_sem.at[len(local) + 2]).start()
            else:
                new = base[s] + acc * rden[s]
                state[s] = new
                blocks[it + 1][s] = new.astype(jnp.bfloat16)
                spread(it + 1, s)

        for s in range(per):
            one_slot(s)

    last_copy.wait()
    pltpu.make_async_copy(change, change_hbm, local_sem.at[len(local) + 2]).wait()
    for copy in sent:
        copy.wait_send()
    for it in range(ITERS):
        arrived(gath[it][0].at[pl.ds(0, group - per)], x_send.at[it])
        sends = recv[it].at[pl.ds(0, (PLANE - 1) * NZ // NX)]
        arrived(sends, y_send.at[it])


def body(amplitudes, integrals, energies, intersections, couplings, projector, pair_orbitals, coupled, pair_slot):
    per, width, _ = amplitudes.shape
    nb = coupled.shape[1]
    total = pair_slot.shape[0]
    group = NX * per
    quarter = width // NX
    bf16, f32, i32 = jnp.bfloat16, jnp.float32, jnp.int32
    smem = pl.BlockSpec(memory_space=pltpu.SMEM)
    hbm = pl.BlockSpec(memory_space=pltpu.HBM)
    dma = pltpu.SemaphoreType.DMA
    square = (per, width, width)
    share = NOCC // NC
    scratch = [pltpu.VMEM((group, quarter, width), bf16) for _ in range(2 * NZ)]
    scratch += [pltpu.VMEM((PLANE, NZ, quarter, width), bf16) for _ in range(2)]
    scratch += [pltpu.VMEM((NZ * NY * NC, width, width), bf16) for _ in range(2)]
    scratch += [pltpu.VMEM(square, bf16) for _ in range(2)]
    scratch += [
        pltpu.VMEM((ITERS, NOCC, width), f32),
        pltpu.VMEM((ITERS, NOCC, width), f32),
        pltpu.VMEM((2 * ITERS, share, width), f32),
        pltpu.VMEM((ITERS, NY - 1, share, width), f32),
        pltpu.VMEM((ITERS, NX - 1, share, width), f32),
        pltpu.VMEM((ITERS, NZ, share, width), f32),
        pltpu.VMEM((ITERS, 4, share, width), f32),
        pltpu.VMEM((per * nb, width, width), bf16),
        pltpu.VMEM(square, bf16),
        pltpu.VMEM(square, f32),
        pltpu.VMEM((per, width), f32),
        pltpu.VMEM((per, width), f32),
        pltpu.VMEM((nb, total), i32),
        pltpu.VMEM((total // width, width), i32),
        pltpu.VMEM(square, f32),
        pltpu.VMEM(square, f32),
        pltpu.VMEM(square, f32),
        pltpu.VMEM(square, f32),
        pltpu.VMEM(square, f32),
        pltpu.VMEM((NZ, width), i32),
        pltpu.VMEM((nb, width), i32),
        pltpu.SMEM((NZ, width), i32),
        pltpu.SMEM((nb, width), i32),
        pltpu.SMEM((per * nb,), i32),
        pltpu.SMEM((per, nb), f32),
        pltpu.SMEM((2, per), i32),
        pltpu.SMEM((total,), i32),
        dma((14,)),
        dma((ITERS,)),
        dma((ITERS,)),
        dma((ITERS, NX * NZ)),
        dma((ITERS,)),
        dma((ITERS,)),
        dma((ITERS, 5)),
        dma((ITERS, NZ + 4)),
    ]
    last, change = pl.pallas_call(
        kernel,
        out_shape=(
            jax.ShapeDtypeStruct(square, f32),
            jax.ShapeDtypeStruct(square, f32),
        ),
        in_specs=[hbm, hbm, hbm, hbm, hbm, hbm, hbm, hbm, hbm, hbm],
        out_specs=(hbm, hbm),
        scratch_shapes=scratch,
        compiler_params=pltpu.CompilerParams(
            collective_id=0, has_side_effects=True, vmem_limit_bytes=67043328
        ),
    )(
        couplings,
        pair_orbitals.T,
        pair_slot,
        amplitudes,
        integrals,
        energies,
        intersections.reshape(per * nb, width, width),
        projector,
        coupled.T,
        pair_slot.reshape(total // width, width),
    )
    denom = energies[:, :, None] + energies[:, None, :]
    residual = integrals.astype(f32) + denom * last + change
    return (last - residual / denom, residual)


def solution(mesh):
    both = ("pairs", "orb")
    return jax.shard_map(
        body,
        mesh=mesh,
        in_specs=(
            P(both, None, None),
            P(both, None, None),
            P(both, None),
            P(both, None, None, None),
            P(both, None),
            P(both, None),
            P(both, None),
            P(),
            P(),
        ),
        out_specs=(P(both, None, None), P(both, None, None)),
        check_vma=False,
    )
```
